32 devices in a mesh: blk: 4 (over y, core), dp: 8 (over z, x).
Axes of the slice: x: 2, y: 2, z: 4, core: 2. Of those that a mesh axis runs over, the one named last changes fastest.
Arguments:
- tokens: bfloat16 [16, 4, 512, 768], P('dp', 'blk'), may hold values from -6 to 6
- cotangent: bfloat16 [16, 4, 512, 768], P('dp', 'blk'), may hold values from -6 to 6
- lengths: int32 [16, 2], P('dp'), may hold values from 513 to 1024, as said below
- head_mode: int32 [12], replicated, may hold values from 0 to 1, as said below
- w_query: bfloat16 [589824], P(('blk', 'dp')), may hold values from -0.21875 to 0.21875
- w_key: bfloat16 [589824], P(('blk', 'dp')), may hold values from -0.21875 to 0.21875
- w_value: bfloat16 [589824], P(('blk', 'dp')), may hold values from -0.21875 to 0.21875
- w_out: bfloat16 [589824], P(('blk', 'dp')), may hold values from -0.875 to 0.875
- w_up: bfloat16 [2359296], P(('blk', 'dp')), may hold values from -0.21875 to 0.21875
- w_down: bfloat16 [2359296], P(('blk', 'dp')), may hold values from -0.109375 to 0.109375
- b_up: bfloat16 [3072], P(('blk', 'dp')), may hold values from -3 to 3
- vectors: bfloat16 [6144], P(('blk', 'dp'))
Outputs:
- activations: bfloat16 [16, 4, 512, 768], P('dp', 'blk')
- input_grad: float32 [16, 4, 512, 768], P('dp', 'blk')
- grad_query: float32 [589824], P(('blk', 'dp'))
- grad_key: float32 [589824], P(('blk', 'dp'))
- grad_value: float32 [589824], P(('blk', 'dp'))
- grad_out: float32 [589824], P(('blk', 'dp'))
- grad_up: float32 [2359296], P(('blk', 'dp'))
- grad_down: float32 [2359296], P(('blk', 'dp'))
- grad_up_bias: float32 [3072], P(('blk', 'dp'))
- grad_vectors: float32 [6144], P(('blk', 'dp'))
The draws below stay inside these ranges and needn't reach their ends.
Inputs may be any that keep to these rules, and one draw needn't show every extreme that they name: `lengths`: key positions at or past a sequence's length are padding. `head_mode`: exactly 6 heads are marked 1.
All inputs are finite; a program needn't handle non-finite values.
Results may differ from the reference program's by a relative error of at most 0.013.
The reference program's roundings to bfloat16 on the way count: a program that leaves them out, or rounds other values in their place, can miss the bound.
Values may be sent and summed in bfloat16 or wider, within the bound.
No kernel may reach another device: no remote copies, remote signals or barrier semaphores. Data moves between devices by JAX's collectives and lax.ppermute only.
A program may use at most 192 MiB of HBM per device.

```python
import jax
import jax.numpy as jnp
from jax import lax

D = 768
H = 12
HD = 64
FF = 3072
BLOCK = 512
GROUPS = 16
N_BLK = 4


def draw_lengths(key, part):
    offsets = jax.random.randint(key, (GROUPS, 2), 0, BLOCK)
    cut_back = offsets * offsets // BLOCK
    result = 2 * BLOCK - cut_back
    result = result.at[0, 0].set(2 * BLOCK)
    result = result.at[0, 1].set(BLOCK + 1)
    return result.astype(jnp.int32)


def draw_head_mode(key, part):
    ordering = jax.random.permutation(jax.random.fold_in(key, 7919), H)
    return (ordering < H // 2).astype(jnp.int32)


def draw_vectors(key, part):
    base = jnp.clip(jax.random.normal(key, (8, D), jnp.float32), -4.0, 4.0)
    spreads = jnp.array([0.5, 0.5, 0.5, 0.15, 0.5, 0.5, 0.15, 0.5], jnp.float32)[:, None]
    centres = jnp.array([0.0, 0.0, 0.0, 1.0, 0.0, 0.0, 1.0, 0.0], jnp.float32)[:, None]
    return (centres + spreads * base).reshape(8 * D).astype(jnp.bfloat16)


def spiked(values, rng, source, target, parts, factor):
    owner, partner = [(jnp.arange(values.shape[axis_at]) // (values.shape[axis_at] // parts)).reshape([-1 if axis == axis_at else 1 for axis in range(values.ndim)]) for axis_at in (source, target)]
    chosen = jax.random.permutation(rng, parts)[partner]
    strong = (owner == chosen) | (owner == (partner + parts // 2) % parts)
    return jnp.where(strong, factor * values, values)


def shard_levels(key, dims, pieces, low, largest):
    level, own = 1.0, jax.random.fold_in(key, 6)
    for axis_at, parts in pieces:
        steps = jnp.exp(jax.random.uniform(jax.random.fold_in(own, axis_at), (parts,), jnp.float32, low / len(pieces), largest / len(pieces)))
        level = level * jnp.repeat(steps, dims[axis_at] // parts).reshape([-1 if axis == axis_at else 1 for axis in range(len(dims))])
    return level


def scatter_about(rng, extent, scale, limit, cuts=(), kind=jnp.bfloat16):
    loudness = shard_levels(rng, extent, cuts, -0.22, 0.18) if cuts else 1.0
    drawn = jax.random.normal(rng, extent, jnp.float32) * scale * loudness
    return jnp.minimum(jnp.maximum(drawn, -limit), limit).astype(kind)


def heavy_noise(stream_key, dims, scale, most, cuts, heavy, held_as=jnp.bfloat16):
    values = scale * jax.random.normal(stream_key, dims, jnp.float32)
    if cuts:
        values = values * shard_levels(stream_key, dims, cuts, -0.22, 0.18)
    return jnp.clip(spiked(values, jax.random.fold_in(stream_key, 3), *heavy), -most, most).astype(held_as)


def setup_inputs(seed: int = 0) -> dict:
    key_of = jax.random.split(jax.random.key(seed), 13)
    return {
        "tokens": heavy_noise(key_of[0], (GROUPS, N_BLK, BLOCK, D), 1.0, 6.0, ((0, 8), (1, 4)), (0, 3, 8, 2.0)),
        "cotangent": scatter_about(key_of[1], (GROUPS, N_BLK, BLOCK, D), 1.0, 6.0, ((0, 8), (1, 4))),
        "lengths": draw_lengths(jax.random.fold_in(key_of[12], 71), 0),
        "head_mode": draw_head_mode(jax.random.fold_in(key_of[12], 71), 0),
        "w_query": scatter_about(key_of[4], (D * D,), D ** -0.5, 0.21875, ((0, 32),)),
        "w_key": scatter_about(key_of[5], (D * D,), D ** -0.5, 0.21875, ((0, 32),)),
        "w_value": scatter_about(key_of[6], (D * D,), D ** -0.5, 0.21875, ((0, 32),)),
        "w_out": scatter_about(key_of[7], (D * D,), (D // 16) ** -0.5, 0.875, ((0, 32),)),
        "w_up": scatter_about(key_of[8], (D * FF,), D ** -0.5, 0.21875, ((0, 32),)),
        "w_down": scatter_about(key_of[9], (FF * D,), FF ** -0.5, 0.109375, ((0, 32),)),
        "b_up": scatter_about(key_of[10], (FF,), 0.5, 3.0, ((0, 32),)),
        "vectors": draw_vectors(jax.random.fold_in(key_of[12], 71), 0),
    }


highest = lax.Precision.HIGHEST
norm_eps = 1e-05
masked_fill = -1000000000.0

@jax.custom_vjp
def low(v):
    return lax.optimization_barrier(v.astype(jnp.bfloat16)).astype(jnp.float32)

@jax.custom_vjp
def low_back(v):
    return v

def low_keep(v):
    return (low(v), None)

def low_pass(kept, grad):
    return (grad,)

def back_keep(v):
    return (v, None)

def back_low(kept, grad):
    return (low(grad),)
low.defvjp(low_keep, low_pass)
low_back.defvjp(back_keep, back_low)

def layer_norm(inputs, gain_row, bias_row):
    average = lax.optimization_barrier(jnp.mean(inputs, axis=-1, keepdims=True))
    centred = inputs - average
    variance = lax.optimization_barrier(jnp.mean(centred * centred, axis=-1, keepdims=True))
    return centred * lax.rsqrt(variance + norm_eps) * gain_row + bias_row

def product(left_side, right_side):
    return jnp.dot(left_side, right_side, precision=highest)

def sequence_layer(sequence, seq_length, head_mode, params):
    mat_query, mat_key, mat_value, mat_out, mat_up, mat_down, up_bias, vec_rows = params
    inputs = sequence.reshape(2 * BLOCK, D)
    queries = low_back(low(product(inputs, mat_query) + vec_rows[0]))
    key_rows = low_back(low(product(inputs, mat_key)))
    value_rows = low_back(low(product(inputs, mat_value) + vec_rows[1]))
    queries = queries.reshape(2, BLOCK, H, HD)
    key_rows = key_rows.reshape(2, BLOCK, H, HD)
    value_rows = value_rows.reshape(2, BLOCK, H, HD)
    swapped = (head_mode == 1)[None, None, :, None]
    key_used = jnp.where(swapped, key_rows[::-1], key_rows)
    value_used = jnp.where(swapped, value_rows[::-1], value_rows)
    block_ids = jnp.arange(2, dtype=jnp.int32)[:, None]
    key_start = jnp.where(head_mode[None, :] == 1, 1 - block_ids, block_ids) * BLOCK
    position = key_start[:, :, None] + jnp.arange(BLOCK, dtype=jnp.int32)[None, None, :]
    key_valid = position < seq_length
    scores = jnp.einsum('bqhd,bkhd->bhqk', queries, key_used, precision=highest) * HD ** (-0.5)
    scores = low_back(jnp.where(key_valid[:, :, None, :], scores, masked_fill))
    attn_probs = low(jax.nn.softmax(scores, axis=-1))
    context = jnp.einsum('bhqk,bkhd->bqhd', attn_probs, value_used, precision=highest)
    context = low_back(low(context.reshape(2 * BLOCK, D)))
    branch = low_back(product(context, mat_out) + vec_rows[2])
    normed_first = layer_norm(inputs + branch, vec_rows[3], vec_rows[4])
    hidden = low_back(product(low(normed_first), mat_up) + up_bias)
    activated = low(jax.nn.gelu(hidden, approximate=False))
    second = low_back(product(activated, mat_down) + vec_rows[5])
    output = layer_norm(normed_first + second, vec_rows[6], vec_rows[7])
    return output.reshape(2, BLOCK, D)

def reference(tokens, cotangent, lengths, head_mode, w_query, w_key, w_value, w_out, w_up, w_down, b_up, vectors):

    def forward(tokens_f, query_flat, key_flat, value_flat, out_flat, up_flat, down_flat, up_bias, vector_flat):
        params = (query_flat.reshape(D, D), key_flat.reshape(D, D), value_flat.reshape(D, D), out_flat.reshape(D, D), up_flat.reshape(D, FF), down_flat.reshape(FF, D), up_bias, vector_flat.reshape(8, D))

        def group_layer(bundle):
            group_tokens, group_lengths = bundle
            front_half = sequence_layer(group_tokens[0:2], group_lengths[0], head_mode, params)
            back_half = sequence_layer(group_tokens[2:4], group_lengths[1], head_mode, params)
            return jnp.concatenate([front_half, back_half], axis=0)
        return lax.map(jax.checkpoint(group_layer), (tokens_f, lengths))
    inputs_f = tuple((argument.astype(jnp.float32) for argument in (tokens, w_query, w_key, w_value, w_out, w_up, w_down, b_up, vectors)))
    output, pullback = jax.vjp(forward, *inputs_f)
    gradients = pullback(cotangent.astype(jnp.float32))
    return (output.astype(jnp.bfloat16), gradients[0], gradients[1], gradients[2], gradients[3], gradients[4], gradients[5], gradients[6], gradients[7], gradients[8])
```

```python
from functools import partial

import jax
import jax.numpy as jnp
from jax import lax
from jax.experimental import pallas as pl
from jax.experimental.pallas import tpu as pltpu
from jax.sharding import PartitionSpec as P

D = 768
H = 12
HD = 64
FF = 3072
BLOCK = 512
HALF = D // 2
PAIR = 2 * HD
LANES = 128
GROUPS_W = 32
ROWS = D // GROUPS_W

norm_eps = 1e-05
masked_fill = -1000000000.0
LOG2E = 1.4426950408889634
SQRT_HALF = 0.7071067811865476
INV_SQRT_2PI = 0.3989422804014327

bf16 = jnp.bfloat16
f32 = jnp.float32
BOTH = ("blk", "dp")


def partner(value, axis, distance):
    mask = 2**distance
    pairs = [(source, source ^ mask) for source in range(lax.axis_size(axis))]
    return lax.ppermute(value, axis, pairs)


def dot_nn(a, b):
    return lax.dot_general(a, b, (((1,), (0,)), ((), ())), preferred_element_type=f32)


def dot_nt(a, b):
    return lax.dot_general(a, b, (((1,), (1,)), ((), ())), preferred_element_type=f32)


def dot_tn(a, b):
    return lax.dot_general(a, b, (((0,), (0,)), ((), ())), preferred_element_type=f32)


def whole(shape):
    return pl.BlockSpec(shape, lambda *_: (0,) * len(shape))


def call(body, grid, in_specs, out_specs, out_shape, scratch=(), prefetch=0, flops=0, moved=0, name=None):
    return pl.pallas_call(
        body,
        grid_spec=pltpu.PrefetchScalarGridSpec(
            num_scalar_prefetch=prefetch,
            grid=grid,
            in_specs=in_specs,
            out_specs=out_specs,
            scratch_shapes=list(scratch),
        ),
        out_shape=out_shape,
        compiler_params=pltpu.CompilerParams(vmem_limit_bytes=60 * 1024 * 1024),
        cost_estimate=pl.CostEstimate(flops=flops, bytes_accessed=moved, transcendentals=0),
        name=name,
    )


def sds(shape, dtype):
    return jax.ShapeDtypeStruct(shape, dtype)


def square(ref):
    return ref[...].reshape(D, D)


def project_body(x_ref, xp_ref, wq_ref, wk_ref, wv_ref, bias_ref, q_ref, k_ref, v_ref):
    own, other = x_ref[...], xp_ref[...]
    q_ref[...] = (dot_nn(own, square(wq_ref)) + bias_ref[0:1, :]).astype(bf16)
    wk, wv = square(wk_ref), square(wv_ref)
    k_ref[:, :HALF] = dot_nn(other, wk[:, :HALF]).astype(bf16)
    k_ref[:, HALF:] = dot_nn(own, wk[:, HALF:]).astype(bf16)
    v_ref[:, :HALF] = (dot_nn(other, wv[:, :HALF]) + bias_ref[1:2, :HALF]).astype(bf16)
    v_ref[:, HALF:] = (dot_nn(own, wv[:, HALF:]) + bias_ref[1:2, HALF:]).astype(bf16)


def project(x, xp, pack, bias):
    rows = x.shape[0]
    step = BLOCK
    row_spec = pl.BlockSpec((step, D), lambda i: (i, 0))
    weight = [pl.BlockSpec((GROUPS_W, ROWS, D), lambda i, s=s: (0, s, 0)) for s in range(3)]
    return call(
        project_body,
        (rows // step,),
        [row_spec, row_spec, *weight, whole((8, D))],
        [row_spec] * 3,
        [sds((rows, D), bf16)] * 3,
        flops=6 * rows * D * D,
        moved=16 * rows * D,
        name="project",
    )(x, xp, pack, pack, pack, bias)


def attend_body(valid_ref, q_ref, k_ref, v_ref, ctx_ref, p_ref):
    seq, pair = pl.program_id(0), pl.program_id(1)
    valid = valid_ref[seq, pair // 3]
    queries, keys, values = q_ref[...], k_ref[...], v_ref[...]
    lane = lax.broadcasted_iota(jnp.int32, (BLOCK, PAIR), 1)
    key_row = lax.broadcasted_iota(jnp.int32, (BLOCK, 1), 0)
    fill = jnp.where(key_row < valid, 0.0, masked_fill * LOG2E)
    parts = []
    for head in range(2):
        mine = (lane < HD) if head == 0 else (lane >= HD)
        masked = jnp.where(mine, queries, jnp.zeros_like(queries))
        scores = dot_nt(keys, masked) * (LOG2E * HD ** (-0.5)) + fill
        top = jnp.max(scores, axis=0, keepdims=True)
        weights = jnp.exp2(scores - top)
        total = jnp.sum(weights, axis=0, keepdims=True)
        probs = (weights * (1.0 / total)).astype(bf16)
        p_ref[0, head] = probs
        parts.append(dot_tn(probs, values))
    ctx_ref[...] = jnp.where(lane < HD, parts[0], parts[1]).astype(bf16)


def attend(valid, q, k, v):
    rows = q.shape[0]
    seqs = rows // BLOCK
    spec = pl.BlockSpec((BLOCK, PAIR), lambda s, j, *_: (s, j))
    return call(
        attend_body,
        (seqs, H // 2),
        [spec] * 3,
        [spec, pl.BlockSpec((1, 2, BLOCK, BLOCK), lambda s, j, *_: (s, j, 0, 0))],
        [sds((rows, D), bf16), sds((seqs, H, BLOCK, BLOCK), bf16)],
        prefetch=1,
        flops=16 * rows * BLOCK * D,
        moved=8 * rows * D + 2 * rows * H * BLOCK,
        name="attend",
    )(valid, q, k, v)


def attend_back_body(q_ref, k_ref, v_ref, p_ref, gctx_ref, delta_ref, out_ref):
    pair = pl.program_id(1)
    queries, keys, values, grad_ctx = q_ref[...], k_ref[...], v_ref[...], gctx_ref[...]
    lane = lax.broadcasted_iota(jnp.int32, (BLOCK, PAIR), 1)
    scale = HD ** (-0.5)
    gq, gk, gv = [], [], []
    for head in range(2):
        mine = (lane < HD) if head == 0 else (lane >= HD)
        probs = p_ref[0, head]
        delta = delta_ref[pl.ds(2 * pair + head, 1), :]
        grad_probs = dot_nt(jnp.where(mine, values, jnp.zeros_like(values)), grad_ctx)
        grad_scores = (probs.astype(f32) * (grad_probs - delta)).astype(bf16)
        gv.append(dot_nn(probs, grad_ctx))
        gk.append(dot_nn(grad_scores, queries))
        gq.append(dot_tn(grad_scores, keys))
    first = lane < HD
    out_ref[0] = (jnp.where(first, gq[0], gq[1]) * scale).astype(bf16)
    out_ref[1] = (jnp.where(first, gk[0], gk[1]) * scale).astype(bf16)
    out_ref[2] = jnp.where(first, gv[0], gv[1]).astype(bf16)


def attend_back(q, k, v, probs, grad_ctx, delta):
    rows = q.shape[0]
    seqs = rows // BLOCK
    spec = pl.BlockSpec((BLOCK, PAIR), lambda s, j: (s, j))
    return call(
        attend_back_body,
        (seqs, H // 2),
        [spec] * 3
        + [
            pl.BlockSpec((1, 2, BLOCK, BLOCK), lambda s, j: (s, j, 0, 0)),
            spec,
            pl.BlockSpec((16, BLOCK), lambda s, j: (0, s)),
        ],
        pl.BlockSpec((3, BLOCK, PAIR), lambda s, j: (0, s, j)),
        sds((3, rows, D), bf16),
        flops=32 * rows * BLOCK * D,
        moved=14 * rows * D + 2 * rows * H * BLOCK,
        name="attend_back",
    )(q, k, v, probs, grad_ctx, delta)


def mean_last(value):
    return jnp.sum(value, axis=-1, keepdims=True) * (1.0 / D)


def first_norm_body(ctx_ref, x_ref, wo_ref, order_ref, vec_ref, hat_ref, inv_ref, low_ref, wop_ref, wo_scr):
    @pl.when(pl.program_id(0) == 0)
    def _():
        permuted = dot_tn(order_ref[...], square(wo_ref)).astype(bf16)
        wo_scr[...] = permuted
        wop_ref[...] = permuted

    branch = dot_nn(ctx_ref[...], wo_scr[...]) + vec_ref[2:3, :]
    residual = x_ref[...].astype(f32) + branch
    centred = residual - mean_last(residual)
    inv = lax.rsqrt(mean_last(centred * centred) + norm_eps)
    hat = centred * inv
    hat_ref[...] = hat
    inv_ref[...] = jnp.broadcast_to(inv, inv_ref.shape)
    low_ref[...] = (hat * vec_ref[3:4, :] + vec_ref[4:5, :]).astype(bf16)


def first_norm(ctx, x, pack, order, vecs):
    rows = x.shape[0]
    step = 256
    row_spec = pl.BlockSpec((step, D), lambda i: (i, 0))
    return call(
        first_norm_body,
        (rows // step,),
        [
            row_spec,
            row_spec,
            pl.BlockSpec((GROUPS_W, ROWS, D), lambda i: (0, 8, 0)),
            whole((D, D)),
            whole((8, D)),
        ],
        [row_spec, pl.BlockSpec((step, LANES), lambda i: (i, 0)), row_spec, whole((D, D))],
        [sds((rows, D), f32), sds((rows, LANES), f32), sds((rows, D), bf16), sds((D, D), bf16)],
        scratch=[pltpu.VMEM((D, D), bf16)],
        flops=2 * rows * D * D,
        moved=12 * rows * D,
        name="first_norm",
    )(ctx, x, pack, order, vecs)


def gelu_and_slope(value):
    size = jnp.abs(value)
    gauss = jnp.exp2(value * value * (-0.5 * LOG2E))
    knot = 1.0 / (1.0 + size * (0.3275911 * SQRT_HALF))
    poly = knot * (
        0.254829592 + knot * (-0.284496736 + knot * (1.421413741 + knot * (-1.453152027 + knot * 1.061405429)))
    )
    tail = 0.5 * poly * gauss
    normal_cdf = jnp.where(value >= 0.0, 1.0 - tail, tail)
    return value * normal_cdf, normal_cdf + value * gauss * INV_SQRT_2PI


def ffn_forward_body(
    low_ref, hat_ref, cot_ref, up_ref, down_ref, bias_ref, vec_ref,
    act_ref, slope_ref, out_ref, gtwo_ref, gsec_ref, sums_ref, acc,
):
    chunk, last = pl.program_id(1), pl.num_programs(1) - 1
    first = (pl.program_id(0) == 0) & (chunk == 0)
    rows = low_ref.shape[0]
    step = 256
    w_up = square(up_ref)
    w_down = square(down_ref)

    @pl.when(first)
    def _():
        sums_ref[...] = jnp.zeros_like(sums_ref)

    for start in range(0, rows, step):
        part = pl.ds(start, step)
        hidden = dot_nn(low_ref[part, :], w_up) + bias_ref[0]
        activated, slope = gelu_and_slope(hidden)
        activated = activated.astype(bf16)
        act_ref[part, :] = activated
        slope_ref[part, :] = slope.astype(bf16)
        down = dot_nn(activated, w_down)

        @pl.when(chunk == 0)
        def _():
            acc[part, :] = down

        @pl.when(chunk > 0)
        def _():
            acc[part, :] += down

    @pl.when(chunk == last)
    def _():
        gain, bias = vec_ref[6:7, :], vec_ref[7:8, :]

        def rows_of(index, sums):
            part = pl.ds(pl.multiple_of(index * step, step), step)
            residual = hat_ref[part, :] * vec_ref[3:4, :] + vec_ref[4:5, :] + (acc[part, :] + vec_ref[5:6, :])
            centred = residual - mean_last(residual)
            inv = lax.rsqrt(mean_last(centred * centred) + norm_eps)
            hat = centred * inv
            out_ref[part, :] = (hat * gain + bias).astype(bf16)
            cot = cot_ref[part, :].astype(f32)
            scaled = cot * gain
            grad = inv * (scaled - mean_last(scaled) - hat * mean_last(scaled * hat))
            gtwo_ref[part, :] = grad
            low = grad.astype(bf16)
            gsec_ref[part, :] = low
            return (
                sums[0] + jnp.sum(cot * hat, axis=0, keepdims=True),
                sums[1] + jnp.sum(cot, axis=0, keepdims=True),
                sums[2] + jnp.sum(low.astype(f32), axis=0, keepdims=True),
            )

        zero = jnp.zeros((1, D), f32)
        sums = lax.fori_loop(0, rows // step, rows_of, (zero, zero, zero))
        for index, value in enumerate(sums):
            sums_ref[index : index + 1, :] += value


def ffn_forward(low, hat, cot, pack, up_bias, vecs):
    rows = low.shape[0]
    span = 1024
    chunks = FF // D
    row_spec = pl.BlockSpec((span, D), lambda r, c: (r, 0))
    wide = pl.BlockSpec((span, D), lambda r, c: (r, c))
    return call(
        ffn_forward_body,
        (rows // span, chunks),
        [
            row_spec,
            row_spec,
            row_spec,
            pl.BlockSpec((GROUPS_W, ROWS, D), lambda r, c: (0, 4 + c, 0)),
            pl.BlockSpec((GROUPS_W // 4, 4 * ROWS, D), lambda r, c: (c, 0, 0)),
            pl.BlockSpec((1, 1, D), lambda r, c: (c, 0, 0)),
            whole((8, D)),
        ],
        [wide, wide, row_spec, row_spec, row_spec, whole((8, D))],
        [
            sds((rows, FF), bf16),
            sds((rows, FF), bf16),
            sds((rows, D), bf16),
            sds((rows, D), f32),
            sds((rows, D), bf16),
            sds((8, D), f32),
        ],
        scratch=[pltpu.VMEM((span, D), f32)],
        flops=4 * rows * D * FF,
        moved=26 * rows * D + 4 * D * FF,
        name="ffn_forward",
    )(low, hat, cot, pack, pack, up_bias, vecs)


def grad_down_body(act_ref, gsec_ref, out_ref):
    out_ref[...] = dot_tn(act_ref[...], gsec_ref[...]).astype(bf16).reshape(out_ref.shape)


def grad_down_of(act, gsec):
    rows = act.shape[0]
    return call(
        grad_down_body,
        (FF // D,),
        [pl.BlockSpec((rows, D), lambda c: (0, c)), whole((rows, D))],
        pl.BlockSpec((GROUPS_W // 4, 4 * ROWS, D), lambda c: (c, 0, 0)),
        sds((GROUPS_W, 4 * ROWS, D), bf16),
        flops=2 * rows * D * FF,
        moved=10 * rows * D + 2 * D * FF,
        name="grad_down",
    )(act, gsec)


def ffn_backward_body(gsec_ref, slope_ref, low_ref, up_ref, down_ref, gup_ref, gbias_ref, acc_ref):
    chunk = pl.program_id(0)
    grad_act = dot_nt(gsec_ref[...], square(down_ref))
    grad_hidden = (grad_act * slope_ref[...].astype(f32)).astype(bf16)
    gbias_ref[0] = jnp.sum(grad_hidden.astype(f32), axis=0, keepdims=True)
    gup_ref[...] = dot_tn(low_ref[...], grad_hidden).astype(bf16).reshape(gup_ref.shape)
    back = dot_nt(grad_hidden, square(up_ref))

    @pl.when(chunk == 0)
    def _():
        acc_ref[...] = back

    @pl.when(chunk > 0)
    def _():
        acc_ref[...] += back


def ffn_backward(gsec, slope, low, pack):
    rows = gsec.shape[0]
    return call(
        ffn_backward_body,
        (FF // D,),
        [
            whole((rows, D)),
            pl.BlockSpec((rows, D), lambda c: (0, c)),
            whole((rows, D)),
            pl.BlockSpec((GROUPS_W, ROWS, D), lambda c: (0, 4 + c, 0)),
            pl.BlockSpec((GROUPS_W // 4, 4 * ROWS, D), lambda c: (c, 0, 0)),
        ],
        [
            pl.BlockSpec((GROUPS_W, ROWS, D), lambda c: (0, c, 0)),
            pl.BlockSpec((1, 1, D), lambda c: (c, 0, 0)),
            whole((rows, D)),
        ],
        [sds((GROUPS_W, 4 * ROWS, D), bf16), sds((FF // D, 1, D), f32), sds((rows, D), f32)],
        flops=6 * rows * D * FF,
        moved=16 * rows * D + 6 * D * FF,
        name="ffn_backward",
    )(gsec, slope, low, pack, pack)


def first_back_body(
    acc_ref, gtwo_ref, hat_ref, inv_ref, ctx_ref, wop_ref, order_ref, vec_ref,
    gres_ref, gctx_ref, gout_ref, delta_ref, sums_ref, gout_scr,
):
    index, last = pl.program_id(0), pl.num_programs(0) - 1
    hat = hat_ref[...]
    inv = inv_ref[:, 0:1]
    grad_first = gtwo_ref[...] + acc_ref[...]
    scaled = grad_first * vec_ref[3:4, :]
    grad = inv * (scaled - mean_last(scaled) - hat * mean_last(scaled * hat))
    gres_ref[...] = grad
    low = grad.astype(bf16)
    ctx = ctx_ref[...]
    grad_ctx = dot_nt(low, wop_ref[...]).astype(bf16)
    gctx_ref[...] = grad_ctx
    head = lax.broadcasted_iota(jnp.int32, (16, D), 0)
    owner = lax.broadcasted_iota(jnp.int32, (16, D), 1) // HD
    chooser = jnp.where(head == owner, 1.0, 0.0).astype(f32)
    product = grad_ctx.astype(f32) * ctx.astype(f32)
    delta_ref[...] = lax.dot_general(
        chooser, product, (((1,), (1,)), ((), ())), preferred_element_type=f32, precision=lax.Precision.HIGHEST
    )
    grad_out = dot_tn(ctx, low)

    @pl.when(index == 0)
    def _():
        gout_scr[...] = grad_out
        sums_ref[...] = jnp.zeros_like(sums_ref)

    @pl.when(index > 0)
    def _():
        gout_scr[...] += grad_out

    sums_ref[0:1, :] += jnp.sum(grad_first * hat, axis=0, keepdims=True)
    sums_ref[1:2, :] += jnp.sum(grad_first, axis=0, keepdims=True)
    sums_ref[2:3, :] += jnp.sum(low.astype(f32), axis=0, keepdims=True)

    @pl.when(index == last)
    def _():
        ordered = dot_nn(order_ref[...], gout_scr[...].astype(bf16))
        gout_ref[...] = ordered.astype(bf16).reshape(gout_ref.shape)


def first_back(acc, gtwo, hat, inv, ctx, wop, order, vecs):
    rows = acc.shape[0]
    step = 256
    row_spec = pl.BlockSpec((step, D), lambda i: (i, 0))
    return call(
        first_back_body,
        (rows // step,),
        [
            row_spec,
            row_spec,
            row_spec,
            pl.BlockSpec((step, LANES), lambda i: (i, 0)),
            row_spec,
            whole((D, D)),
            whole((D, D)),
            whole((8, D)),
        ],
        [
            row_spec,
            row_spec,
            whole((GROUPS_W, ROWS, D)),
            pl.BlockSpec((16, step), lambda i: (0, i)),
            whole((8, D)),
        ],
        [
            sds((rows, D), f32),
            sds((rows, D), bf16),
            sds((GROUPS_W, ROWS, D), bf16),
            sds((16, rows), f32),
            sds((8, D), f32),
        ],
        scratch=[pltpu.VMEM((D, D), f32)],
        flops=4 * rows * D * D,
        moved=20 * rows * D + 6 * D * D,
        name="first_back",
    )(acc, gtwo, hat, inv, ctx, wop, order, vecs)


def grad_project_body(x_ref, xp_ref, grad_ref, out_ref, sums_ref):
    part = pl.program_id(0)
    own = x_ref[...]
    other = jnp.where(part == 0, own, xp_ref[...])
    grad = grad_ref[0]
    left = dot_tn(other, grad[:, :HALF]).astype(bf16)
    right = dot_tn(own, grad[:, HALF:]).astype(bf16)
    out_ref[:, :, :HALF] = left.reshape(GROUPS_W, ROWS, HALF)
    out_ref[:, :, HALF:] = right.reshape(GROUPS_W, ROWS, HALF)
    sums_ref[0] = jnp.broadcast_to(jnp.sum(grad.astype(f32), axis=0, keepdims=True), (8, D))


def grad_project(x, xp, grads):
    rows = x.shape[0]
    return call(
        grad_project_body,
        (3,),
        [whole((rows, D)), whole((rows, D)), pl.BlockSpec((1, rows, D), lambda s: (s, 0, 0))],
        [pl.BlockSpec((GROUPS_W, ROWS, D), lambda s: (0, s, 0)), pl.BlockSpec((1, 8, D), lambda s: (s, 0, 0))],
        [sds((GROUPS_W, 3 * ROWS, D), bf16), sds((3, 8, D), f32)],
        flops=6 * rows * D * D,
        moved=10 * rows * D + 6 * D * D,
        name="grad_project",
    )(x, xp, grads)


def grad_input_body(gres_ref, grads_ref, back_ref, wq_ref, wk_ref, wv_ref, out_ref):
    wk, wv = square(wk_ref), square(wv_ref)
    total = gres_ref[...] + dot_nt(grads_ref[0], square(wq_ref))
    total = total + dot_nt(back_ref[:, :HALF], wk[:, :HALF]) + dot_nt(grads_ref[1][:, HALF:], wk[:, HALF:])
    total = total + dot_nt(back_ref[:, HALF:], wv[:, :HALF]) + dot_nt(grads_ref[2][:, HALF:], wv[:, HALF:])
    out_ref[...] = total


def grad_input_of(gres, grads, back, pack):
    rows = gres.shape[0]
    step = 256
    row_spec = pl.BlockSpec((step, D), lambda i: (i, 0))
    weight = [pl.BlockSpec((GROUPS_W, ROWS, D), lambda i, s=s: (0, s, 0)) for s in range(3)]
    return call(
        grad_input_body,
        (rows // step,),
        [row_spec, pl.BlockSpec((3, step, D), lambda i: (0, i, 0)), row_spec, *weight],
        row_spec,
        sds((rows, D), f32),
        flops=6 * rows * D * D,
        moved=16 * rows * D + 6 * D * D,
        name="grad_input",
    )(gres, grads, back, pack, pack, pack)


def gather(value):
    return lax.all_gather(value, BOTH, axis=0)


def scatter(value):
    return lax.psum_scatter(value, BOTH, scatter_dimension=0)


def joined(gathered, start, rows, columns=1):
    count = gathered.shape[0]
    part = gathered[:, start : start + columns * rows]
    if columns > 1:
        part = part.reshape(GROUPS_W, count // GROUPS_W, columns, rows, D).transpose(0, 2, 1, 3, 4)
    return part.reshape(GROUPS_W, -1, D)


def parted(grouped, count, rows, columns=1):
    if columns > 1:
        grouped = grouped.reshape(GROUPS_W, columns, count // GROUPS_W, rows, D).transpose(0, 2, 1, 3, 4)
    return grouped.reshape(count, columns * rows, D)


def body(tokens, cotangent, lengths, head_mode, w_query, w_key, w_value, w_out, w_up, w_down, b_up, vectors):
    seq_count = tokens.shape[0]
    row_count = seq_count * BLOCK
    devices = lax.axis_size("blk") * lax.axis_size("dp")
    own_rows = D // devices
    blk_index = lax.axis_index("blk")
    block_side = blk_index % 2
    member = blk_index // 2
    seq_lengths = jnp.where(member == 0, lengths[:, 0], lengths[:, 1])
    valid = jnp.stack(
        (
            jnp.clip(seq_lengths - (1 - block_side) * BLOCK, 0, BLOCK),
            jnp.clip(seq_lengths - block_side * BLOCK, 0, BLOCK),
        ),
        axis=1,
    ).astype(jnp.int32)
    swapped = head_mode == 1
    place = jnp.where(swapped, jnp.cumsum(swapped) - 1, H // 2 + jnp.cumsum(~swapped) - 1)
    target = jnp.repeat(place * HD, HD) + jnp.tile(jnp.arange(HD), H)
    order = (target[:, None] == jnp.arange(D)[None, :]).astype(bf16)

    inputs = tokens.reshape(row_count, D)
    other_inputs = partner(inputs, "blk", 0)

    small = jnp.concatenate((vectors, b_up))
    small = jnp.pad(small, (0, D - small.shape[0])).reshape(1, D)
    small = jnp.pad(small, ((0, 7), (0, 0)))
    stacked = jnp.concatenate([w.reshape(own_rows, D) for w in (w_query, w_key, w_value)])
    stacked = dot_nn(stacked, order).astype(bf16)
    attn_all = gather(jnp.concatenate((stacked, small)))
    ffn_all = gather(
        jnp.concatenate(
            (
                w_down.reshape(4 * own_rows, D),
                w_up.reshape(own_rows, 4, D).transpose(1, 0, 2).reshape(4 * own_rows, D),
                w_out.reshape(own_rows, D),
            )
        )
    )
    n_vec, n_bias = vectors.shape[0], b_up.shape[0]
    small_all = attn_all[:, 3 * own_rows, :]
    vec_low = small_all[:, :n_vec].reshape(8, D)
    vecs = vec_low.astype(f32)
    bias_qv = jnp.pad(dot_nn(vec_low[0:2], order), ((0, 6), (0, 0)))
    up_bias = small_all[:, n_vec : n_vec + n_bias].reshape(FF // D, 1, D).astype(f32)
    if devices == GROUPS_W:
        attn_pack, ffn_pack = attn_all, ffn_all
    else:
        attn_pack = jnp.concatenate([joined(attn_all, s * own_rows, own_rows) for s in range(3)], axis=1)
        ffn_pack = jnp.concatenate(
            (
                joined(ffn_all, 0, 4 * own_rows),
                joined(ffn_all, 4 * own_rows, own_rows, 4),
                joined(ffn_all, 8 * own_rows, own_rows),
            ),
            axis=1,
        )

    q, k, v = project(inputs, other_inputs, attn_pack, bias_qv)
    ctx, probs = attend(valid, q, k, v)
    hat, inv, low, out_weight = first_norm(ctx, inputs, ffn_pack, order, vecs)
    act, slope, output, gtwo, gsec, sums_two = ffn_forward(
        low, hat, cotangent.reshape(row_count, D), ffn_pack, up_bias, vecs
    )
    grad_down = grad_down_of(act, gsec)
    grad_up, grad_up_bias, acc = ffn_backward(gsec, slope, low, ffn_pack)
    gres, grad_ctx, grad_out, delta, sums_one = first_back(acc, gtwo, hat, inv, ctx, out_weight, order, vecs)
    grads = attend_back(q, k, v, probs, grad_ctx, delta)
    back = partner(jnp.concatenate((grads[1][:, :HALF], grads[2][:, :HALF]), axis=1), "blk", 0)
    grad_qkv, sums_qkv = grad_project(inputs, other_inputs, grads)
    grad_inputs = grad_input_of(gres, grads, back, attn_pack)

    bias_grads = lax.dot_general(
        jnp.stack((sums_qkv[0, 0], sums_qkv[2, 0])),
        order.astype(f32),
        (((1,), (1,)), ((), ())),
        precision=lax.Precision.HIGHEST,
    )
    grad_vectors = jnp.concatenate(
        (
            bias_grads,
            sums_one[2:3],
            sums_one[0:2],
            sums_two[2:3],
            sums_two[0:2],
        )
    ).reshape(devices, n_vec)
    small_grads = jnp.concatenate((grad_vectors, grad_up_bias.reshape(devices, n_bias)), axis=1)
    small_grads = jnp.pad(small_grads, ((0, 0), (0, D - n_vec - n_bias))).astype(bf16)
    small_grads = jnp.pad(small_grads[:, None, :], ((0, 0), (0, 7), (0, 0)))
    down_sum = scatter(parted(grad_down, devices, 4 * own_rows))
    rest_sum = scatter(
        jnp.concatenate(
            (
                parted(grad_up, devices, own_rows, 4),
                parted(grad_out, devices, own_rows),
                jnp.concatenate(
                    [parted(grad_qkv[:, s * ROWS : (s + 1) * ROWS], devices, own_rows) for s in range(3)], axis=1
                ),
                small_grads,
            ),
            axis=1,
        )
    ).astype(f32)
    up_sum = rest_sum[: 4 * own_rows].reshape(4, own_rows, D).transpose(1, 0, 2)
    out_sum = rest_sum[4 * own_rows : 5 * own_rows]
    qkv_sum = lax.dot_general(
        rest_sum[5 * own_rows : 8 * own_rows],
        order.astype(f32),
        (((1,), (1,)), ((), ())),
        precision=lax.Precision.HIGHEST,
    ).reshape(3, own_rows * D)
    small_sum = rest_sum[8 * own_rows]
    return (
        output.reshape(tokens.shape),
        grad_inputs.reshape(tokens.shape),
        qkv_sum[0],
        qkv_sum[1],
        qkv_sum[2],
        out_sum.reshape(-1),
        up_sum.reshape(-1),
        down_sum.astype(f32).reshape(-1),
        small_sum[n_vec : n_vec + n_bias],
        small_sum[:n_vec],
    )


def solution(mesh):
    flat = P(BOTH)
    block = P("dp", "blk", None, None)
    return jax.shard_map(
        body,
        mesh=mesh,
        in_specs=(block, block, P("dp", None), P(), *([flat] * 8)),
        out_specs=(block, block, *([flat] * 8)),
        check_vma=False,
    )
```

```python
from functools import partial

import jax
import jax.numpy as jnp
from jax import lax
from jax.experimental import pallas as pl
from jax.experimental.pallas import tpu as pltpu
from jax.sharding import PartitionSpec as P

D = 768
H = 12
HD = 64
FF = 3072
BLOCK = 512
HALF = D // 2
PAIR = 2 * HD
LANES = 128
GROUPS_W = 32
ROWS = D // GROUPS_W

norm_eps = 1e-05
masked_fill = -1000000000.0
LOG2E = 1.4426950408889634
SQRT_HALF = 0.7071067811865476
INV_SQRT_2PI = 0.3989422804014327

bf16 = jnp.bfloat16
f32 = jnp.float32
BOTH = ("blk", "dp")


def swap(value, axis, mask):
    return lax.ppermute(value, axis, [(source, source ^ mask) for source in range(lax.axis_size(axis))])


def dot_nn(a, b):
    return lax.dot_general(a, b, (((1,), (0,)), ((), ())), preferred_element_type=f32)


def dot_nt(a, b):
    return lax.dot_general(a, b, (((1,), (1,)), ((), ())), preferred_element_type=f32)


def dot_tn(a, b):
    return lax.dot_general(a, b, (((0,), (0,)), ((), ())), preferred_element_type=f32)


def whole(shape):
    return pl.BlockSpec(shape, lambda *_: (0,) * len(shape))


def call(body, grid, in_specs, out_specs, out_shape, scratch=(), prefetch=0, flops=0, moved=0, name=None):
    return pl.pallas_call(
        body,
        grid_spec=pltpu.PrefetchScalarGridSpec(
            num_scalar_prefetch=prefetch,
            grid=grid,
            in_specs=in_specs,
            out_specs=out_specs,
            scratch_shapes=list(scratch),
        ),
        out_shape=out_shape,
        compiler_params=pltpu.CompilerParams(vmem_limit_bytes=60 * 1024 * 1024),
        cost_estimate=pl.CostEstimate(flops=flops, bytes_accessed=moved, transcendentals=0),
        name=name,
    )


def sds(shape, dtype):
    return jax.ShapeDtypeStruct(shape, dtype)


def square(ref):
    return ref[...].reshape(D, D)


PIECES = [(core, y, x) for core in range(2) for y in range(2) for x in range(2)]


def project_body(me_ref, x_ref, xp_ref, *refs):
    pieces, (q_ref, k_ref, v_ref, w_ref, vec_ref, scr) = refs[: len(PIECES)], refs[len(PIECES) :]

    @pl.when(pl.program_id(0) == 0)
    def _():
        me = me_ref[0]
        total = jnp.zeros((8, D), f32)
        for (core, y, x), piece in zip(PIECES, pieces):
            for z in range(piece.shape[0]):
                group = (16 * y + 8 * core + 2 * z + x) ^ me
                for part in range(3):
                    scr[part, group] = piece[z, part * ROWS : (part + 1) * ROWS, :]
                total = total + piece[z, 3 * ROWS : 3 * ROWS + 8, :].astype(f32)
        vec_ref[...] = total
        for part in range(3):
            w_ref[part] = scr[part].reshape(D, D)

    own, other = x_ref[...], xp_ref[...]
    q_ref[...] = (dot_nn(own, w_ref[0]) + vec_ref[0:1, :]).astype(bf16)
    k_ref[:, :HALF] = dot_nn(other, w_ref[1, :, :HALF]).astype(bf16)
    k_ref[:, HALF:] = dot_nn(own, w_ref[1, :, HALF:]).astype(bf16)
    v_ref[:, :HALF] = (dot_nn(other, w_ref[2, :, :HALF]) + vec_ref[1:2, :HALF]).astype(bf16)
    v_ref[:, HALF:] = (dot_nn(own, w_ref[2, :, HALF:]) + vec_ref[1:2, HALF:]).astype(bf16)


def project(me, x, xp, pieces):
    rows = x.shape[0]
    step = BLOCK
    row_spec = pl.BlockSpec((step, D), lambda i, *_: (i, 0))
    return call(
        project_body,
        (rows // step,),
        [row_spec, row_spec] + [whole(pieces[0].shape)] * len(PIECES),
        [row_spec] * 3 + [whole((3, D, D)), whole((8, D))],
        [sds((rows, D), bf16)] * 3 + [sds((3, D, D), bf16), sds((8, D), f32)],
        scratch=[pltpu.VMEM((3, GROUPS_W, ROWS, D), bf16)],
        prefetch=1,
        flops=6 * rows * D * D,
        moved=10 * rows * D + 12 * D * D,
        name="project",
    )(me, x, xp, *pieces)


def attend_body(valid_ref, q_ref, k_ref, v_ref, ctx_ref, p_ref):
    seq, pair = pl.program_id(0), pl.program_id(1)
    valid = valid_ref[seq, pair // 3]
    queries, keys, values = q_ref[...], k_ref[...], v_ref[...]
    lane = lax.broadcasted_iota(jnp.int32, (BLOCK, PAIR), 1)
    key_row = lax.broadcasted_iota(jnp.int32, (BLOCK, 1), 0)
    fill = jnp.where(key_row < valid, 0.0, masked_fill * LOG2E)
    parts = []
    for head in range(2):
        mine = (lane < HD) if head == 0 else (lane >= HD)
        masked = jnp.where(mine, queries, jnp.zeros_like(queries))
        scores = dot_nt(keys, masked) * (LOG2E * HD ** (-0.5)) + fill
        top = jnp.max(scores, axis=0, keepdims=True)
        weights = jnp.exp2(scores - top)
        total = jnp.sum(weights, axis=0, keepdims=True)
        probs = (weights * (1.0 / total)).astype(bf16)
        p_ref[0, head] = probs
        parts.append(dot_tn(probs, values))
    ctx_ref[...] = jnp.where(lane < HD, parts[0], parts[1]).astype(bf16)


def attend(valid, q, k, v):
    rows = q.shape[0]
    seqs = rows // BLOCK
    spec = pl.BlockSpec((BLOCK, PAIR), lambda s, j, *_: (s, j))
    return call(
        attend_body,
        (seqs, H // 2),
        [spec] * 3,
        [spec, pl.BlockSpec((1, 2, BLOCK, BLOCK), lambda s, j, *_: (s, j, 0, 0))],
        [sds((rows, D), bf16), sds((seqs, H, BLOCK, BLOCK), bf16)],
        prefetch=1,
        flops=16 * rows * BLOCK * D,
        moved=8 * rows * D + 2 * rows * H * BLOCK,
        name="attend",
    )(valid, q, k, v)


def attend_back_body(q_ref, k_ref, v_ref, p_ref, gctx_ref, delta_ref, out_ref, give_ref):
    pair = pl.program_id(1)
    queries, keys, values, grad_ctx = q_ref[...], k_ref[...], v_ref[...], gctx_ref[...]
    lane = lax.broadcasted_iota(jnp.int32, (BLOCK, PAIR), 1)
    scale = HD ** (-0.5)
    gq, gk, gv = [], [], []
    for head in range(2):
        mine = (lane < HD) if head == 0 else (lane >= HD)
        probs = p_ref[0, head]
        delta = delta_ref[pl.ds(2 * pair + head, 1), :]
        grad_probs = dot_nt(jnp.where(mine, values, jnp.zeros_like(values)), grad_ctx)
        grad_scores = (probs.astype(f32) * (grad_probs - delta)).astype(bf16)
        gv.append(dot_nn(probs, grad_ctx))
        gk.append(dot_nn(grad_scores, queries))
        gq.append(dot_tn(grad_scores, keys))
    first = lane < HD
    out_ref[0] = (jnp.where(first, gq[0], gq[1]) * scale).astype(bf16)
    grad_keys = (jnp.where(first, gk[0], gk[1]) * scale).astype(bf16)
    grad_values = jnp.where(first, gv[0], gv[1]).astype(bf16)
    out_ref[1] = grad_keys
    out_ref[2] = grad_values

    @pl.when(pair < H // 4)
    def _():
        give_ref[0] = grad_keys
        give_ref[1] = grad_values


def attend_back(q, k, v, probs, grad_ctx, delta):
    rows = q.shape[0]
    seqs = rows // BLOCK
    spec = pl.BlockSpec((BLOCK, PAIR), lambda s, j: (s, j))
    return call(
        attend_back_body,
        (seqs, H // 2),
        [spec] * 3
        + [
            pl.BlockSpec((1, 2, BLOCK, BLOCK), lambda s, j: (s, j, 0, 0)),
            spec,
            pl.BlockSpec((16, BLOCK), lambda s, j: (0, s)),
        ],
        [
            pl.BlockSpec((3, BLOCK, PAIR), lambda s, j: (0, s, j)),
            pl.BlockSpec((2, BLOCK, PAIR), lambda s, j: (0, s, jnp.minimum(j, H // 4 - 1))),
        ],
        [sds((3, rows, D), bf16), sds((2, rows, HALF), bf16)],
        flops=32 * rows * BLOCK * D,
        moved=14 * rows * D + 2 * rows * H * BLOCK,
        name="attend_back",
    )(q, k, v, probs, grad_ctx, delta)


def mean_last(value):
    return jnp.sum(value, axis=-1, keepdims=True) * (1.0 / D)


def first_norm_body(
    ctx_ref, x_ref, wo_ref, bias_ref, order_ref, vec_ref, hat_ref, inv_ref, low_ref, wop_ref, upb_ref, wo_scr
):
    @pl.when(pl.program_id(0) == 0)
    def _():
        total = jnp.zeros((8, D), f32)
        for group in range(GROUPS_W):
            total = total + bias_ref[group].astype(f32)
        upb_ref[...] = total
        permuted = dot_tn(order_ref[...], square(wo_ref)).astype(bf16)
        wo_scr[...] = permuted
        wop_ref[...] = permuted

    branch = dot_nn(ctx_ref[...], wo_scr[...]) + vec_ref[2:3, :]
    residual = x_ref[...].astype(f32) + branch
    centred = residual - mean_last(residual)
    inv = lax.rsqrt(mean_last(centred * centred) + norm_eps)
    hat = centred * inv
    hat_ref[...] = hat
    inv_ref[...] = jnp.broadcast_to(inv, inv_ref.shape)
    low_ref[...] = (hat * vec_ref[3:4, :] + vec_ref[4:5, :]).astype(bf16)


def first_norm(ctx, x, pack, order, vecs):
    rows = x.shape[0]
    step = 256
    row_spec = pl.BlockSpec((step, D), lambda i: (i, 0))
    return call(
        first_norm_body,
        (rows // step,),
        [
            row_spec,
            row_spec,
            pl.BlockSpec((GROUPS_W, ROWS, D), lambda i: (0, 8, 0)),
            pl.BlockSpec((GROUPS_W, 8, D), lambda i: (0, 27, 0)),
            whole((D, D)),
            whole((8, D)),
        ],
        [row_spec, pl.BlockSpec((step, LANES), lambda i: (i, 0)), row_spec, whole((D, D)), whole((8, D))],
        [
            sds((rows, D), f32),
            sds((rows, LANES), f32),
            sds((rows, D), bf16),
            sds((D, D), bf16),
            sds((8, D), f32),
        ],
        scratch=[pltpu.VMEM((D, D), bf16)],
        flops=2 * rows * D * D,
        moved=12 * rows * D,
        name="first_norm",
    )(ctx, x, pack, pack, order, vecs)


def gelu_and_slope(value):
    size = jnp.abs(value)
    gauss = jnp.exp2(value * value * (-0.5 * LOG2E))
    knot = 1.0 / (1.0 + size * (0.3275911 * SQRT_HALF))
    poly = knot * (
        0.254829592 + knot * (-0.284496736 + knot * (1.421413741 + knot * (-1.453152027 + knot * 1.061405429)))
    )
    tail = 0.5 * poly * gauss
    normal_cdf = jnp.where(value >= 0.0, 1.0 - tail, tail)
    return value * normal_cdf, normal_cdf + value * gauss * INV_SQRT_2PI


def ffn_forward_body(
    low_ref, hat_ref, cot_ref, up_ref, down_ref, bias_ref, vec_ref,
    act_ref, slope_ref, out_ref, gtwo_ref, gsec_ref, sums_ref, acc,
):
    chunk, last = pl.program_id(1), pl.num_programs(1) - 1
    first = (pl.program_id(0) == 0) & (chunk == 0)
    rows = low_ref.shape[0]
    step = 256
    w_up = square(up_ref)
    w_down = square(down_ref)

    @pl.when(first)
    def _():
        sums_ref[...] = jnp.zeros_like(sums_ref)

    for start in range(0, rows, step):
        part = pl.ds(start, step)
        hidden = dot_nn(low_ref[part, :], w_up) + bias_ref[pl.ds(chunk, 1), :]
        activated, slope = gelu_and_slope(hidden)
        activated = activated.astype(bf16)
        act_ref[part, :] = activated
        slope_ref[part, :] = slope.astype(bf16)
        down = dot_nn(activated, w_down)

        @pl.when(chunk == 0)
        def _():
            acc[part, :] = down

        @pl.when(chunk > 0)
        def _():
            acc[part, :] += down

    @pl.when(chunk == last)
    def _():
        gain, bias = vec_ref[6:7, :], vec_ref[7:8, :]

        def rows_of(index, sums):
            part = pl.ds(pl.multiple_of(index * step, step), step)
            residual = hat_ref[part, :] * vec_ref[3:4, :] + vec_ref[4:5, :] + (acc[part, :] + vec_ref[5:6, :])
            centred = residual - mean_last(residual)
            inv = lax.rsqrt(mean_last(centred * centred) + norm_eps)
            hat = centred * inv
            out_ref[part, :] = (hat * gain + bias).astype(bf16)
            cot = cot_ref[part, :].astype(f32)
            scaled = cot * gain
            grad = inv * (scaled - mean_last(scaled) - hat * mean_last(scaled * hat))
            gtwo_ref[part, :] = grad
            low = grad.astype(bf16)
            gsec_ref[part, :] = low
            return (
                sums[0] + jnp.sum(cot * hat, axis=0, keepdims=True),
                sums[1] + jnp.sum(cot, axis=0, keepdims=True),
                sums[2] + jnp.sum(low.astype(f32), axis=0, keepdims=True),
            )

        zero = jnp.zeros((1, D), f32)
        sums = lax.fori_loop(0, rows // step, rows_of, (zero, zero, zero))
        for index, value in enumerate(sums):
            sums_ref[index : index + 1, :] += value


def ffn_forward(low, hat, cot, pack, up_bias, vecs):
    rows = low.shape[0]
    span = 1024
    chunks = FF // D
    row_spec = pl.BlockSpec((span, D), lambda r, c: (r, 0))
    wide = pl.BlockSpec((span, D), lambda r, c: (r, c))
    return call(
        ffn_forward_body,
        (rows // span, chunks),
        [
            row_spec,
            row_spec,
            row_spec,
            pl.BlockSpec((GROUPS_W, ROWS, D), lambda r, c: (0, 4 + c, 0)),
            pl.BlockSpec((GROUPS_W // 4, 4 * ROWS, D), lambda r, c: (c, 0, 0)),
            whole((8, D)),
            whole((8, D)),
        ],
        [wide, wide, row_spec, row_spec, row_spec, whole((8, D))],
        [
            sds((rows, FF), bf16),
            sds((rows, FF), bf16),
            sds((rows, D), bf16),
            sds((rows, D), f32),
            sds((rows, D), bf16),
            sds((8, D), f32),
        ],
        scratch=[pltpu.VMEM((span, D), f32)],
        flops=4 * rows * D * FF,
        moved=26 * rows * D + 4 * D * FF,
        name="ffn_forward",
    )(low, hat, cot, pack, pack, up_bias, vecs)


def grad_down_body(act_ref, gsec_ref, out_ref):
    out_ref[...] = dot_tn(act_ref[...], gsec_ref[...]).astype(bf16).reshape(out_ref.shape)


def grad_down_of(act, gsec):
    rows = act.shape[0]
    return call(
        grad_down_body,
        (FF // D,),
        [pl.BlockSpec((rows, D), lambda c: (0, c)), whole((rows, D))],
        pl.BlockSpec((GROUPS_W // 4, 4 * ROWS, D), lambda c: (c, 0, 0)),
        sds((GROUPS_W, 4 * ROWS, D), bf16),
        flops=2 * rows * D * FF,
        moved=10 * rows * D + 2 * D * FF,
        name="grad_down",
    )(act, gsec)


def apart(scr, me, keep, send):
    def one(index, carry):
        group = (2 * index - jnp.bitwise_and(index, 7)) ^ me
        keep(index, scr[group])
        send(index, scr[group ^ 8])
        return carry

    lax.fori_loop(0, GROUPS_W // 2, one, 0)


def ffn_backward_body(
    me_ref, gsec_ref, slope_ref, low_ref, up_ref, down_ref, keep_ref, send_ref, gbias_ref, acc_ref, scr
):
    chunk = pl.program_id(0)
    grad_act = dot_nt(gsec_ref[...], square(down_ref))
    grad_hidden = (grad_act * slope_ref[...].astype(f32)).astype(bf16)
    gbias_ref[0] = jnp.sum(grad_hidden.astype(f32), axis=0, keepdims=True)
    scr[...] = dot_tn(low_ref[...], grad_hidden).astype(bf16).reshape(scr.shape)

    def keep(index, value):
        keep_ref[index] = value

    def send(index, value):
        send_ref[index] = value

    apart(scr, me_ref[0], keep, send)
    back = dot_nt(grad_hidden, square(up_ref))

    @pl.when(chunk == 0)
    def _():
        acc_ref[...] = back

    @pl.when(chunk > 0)
    def _():
        acc_ref[...] += back


def ffn_backward(me, gsec, slope, low, pack):
    rows = gsec.shape[0]
    half = pl.BlockSpec((GROUPS_W // 2, ROWS, D), lambda c, *_: (0, c, 0))
    return call(
        ffn_backward_body,
        (FF // D,),
        [
            whole((rows, D)),
            pl.BlockSpec((rows, D), lambda c, *_: (0, c)),
            whole((rows, D)),
            pl.BlockSpec((GROUPS_W, ROWS, D), lambda c, *_: (0, 4 + c, 0)),
            pl.BlockSpec((GROUPS_W // 4, 4 * ROWS, D), lambda c, *_: (c, 0, 0)),
        ],
        [half, half, pl.BlockSpec((1, 1, D), lambda c, *_: (c, 0, 0)), whole((rows, D))],
        [sds((GROUPS_W // 2, 4 * ROWS, D), bf16)] * 2 + [sds((FF // D, 1, D), f32), sds((rows, D), f32)],
        scratch=[pltpu.VMEM((GROUPS_W, ROWS, D), bf16)],
        prefetch=1,
        flops=6 * rows * D * FF,
        moved=16 * rows * D + 6 * D * FF,
        name="ffn_backward",
    )(me, gsec, slope, low, pack, pack)


def first_back_body(
    acc_ref, gtwo_ref, hat_ref, inv_ref, ctx_ref, wop_ref, order_ref, vec_ref,
    gres_ref, gctx_ref, gout_ref, delta_ref, sums_ref, gout_scr,
):
    index, last = pl.program_id(0), pl.num_programs(0) - 1
    hat = hat_ref[...]
    inv = inv_ref[:, 0:1]
    grad_first = gtwo_ref[...] + acc_ref[...]
    scaled = grad_first * vec_ref[3:4, :]
    grad = inv * (scaled - mean_last(scaled) - hat * mean_last(scaled * hat))
    gres_ref[...] = grad
    low = grad.astype(bf16)
    ctx = ctx_ref[...]
    grad_ctx = dot_nt(low, wop_ref[...]).astype(bf16)
    gctx_ref[...] = grad_ctx
    head = lax.broadcasted_iota(jnp.int32, (16, D), 0)
    owner = lax.broadcasted_iota(jnp.int32, (16, D), 1) // HD
    chooser = jnp.where(head == owner, 1.0, 0.0).astype(f32)
    product = grad_ctx.astype(f32) * ctx.astype(f32)
    delta_ref[...] = lax.dot_general(
        chooser, product, (((1,), (1,)), ((), ())), preferred_element_type=f32, precision=lax.Precision.HIGHEST
    )
    grad_out = dot_tn(ctx, low)

    @pl.when(index == 0)
    def _():
        gout_scr[...] = grad_out
        sums_ref[...] = jnp.zeros_like(sums_ref)

    @pl.when(index > 0)
    def _():
        gout_scr[...] += grad_out

    sums_ref[0:1, :] += jnp.sum(grad_first * hat, axis=0, keepdims=True)
    sums_ref[1:2, :] += jnp.sum(grad_first, axis=0, keepdims=True)
    sums_ref[2:3, :] += jnp.sum(low.astype(f32), axis=0, keepdims=True)

    @pl.when(index == last)
    def _():
        ordered = dot_nn(order_ref[...], gout_scr[...].astype(bf16))
        gout_ref[...] = ordered.astype(bf16).reshape(gout_ref.shape)


def first_back(acc, gtwo, hat, inv, ctx, wop, order, vecs):
    rows = acc.shape[0]
    step = 256
    row_spec = pl.BlockSpec((step, D), lambda i: (i, 0))
    return call(
        first_back_body,
        (rows // step,),
        [
            row_spec,
            row_spec,
            row_spec,
            pl.BlockSpec((step, LANES), lambda i: (i, 0)),
            row_spec,
            whole((D, D)),
            whole((D, D)),
            whole((8, D)),
        ],
        [
            row_spec,
            row_spec,
            whole((GROUPS_W, ROWS, D)),
            pl.BlockSpec((16, step), lambda i: (0, i)),
            whole((8, D)),
        ],
        [
            sds((rows, D), f32),
            sds((rows, D), bf16),
            sds((GROUPS_W, ROWS, D), bf16),
            sds((16, rows), f32),
            sds((8, D), f32),
        ],
        scratch=[pltpu.VMEM((D, D), f32)],
        flops=4 * rows * D * D,
        moved=20 * rows * D + 6 * D * D,
        name="first_back",
    )(acc, gtwo, hat, inv, ctx, wop, order, vecs)


LAST_ROWS = 4 * ROWS + 8
N_VEC = 8 * D // GROUPS_W
N_BIAS = FF // GROUPS_W


def grad_project_body(
    me_ref, x_ref, xp_ref, grad_ref, gout_ref, one_ref, two_ref, upb_ref, order_ref, keep_ref, send_ref, scr, sums, small
):
    part = pl.program_id(0)
    me = me_ref[0]
    own = x_ref[...]
    other = jnp.where(part == 0, own, xp_ref[...])
    grad = grad_ref[0]
    left = dot_tn(other, grad[:, :HALF]).astype(bf16)
    right = dot_tn(own, grad[:, HALF:]).astype(bf16)
    scr[:, :, :HALF] = left.reshape(GROUPS_W, ROWS, HALF)
    scr[:, :, HALF:] = right.reshape(GROUPS_W, ROWS, HALF)
    sums[pl.ds(part, 1), :] = jnp.sum(grad.astype(f32), axis=0, keepdims=True)

    def place(source, start, size):
        def keep(index, value):
            keep_ref[index, start : start + size, :] = value.astype(bf16)

        def send(index, value):
            send_ref[index, start : start + size, :] = value.astype(bf16)

        apart(source, me, keep, send)

    for index in range(3):

        @pl.when(part == index)
        def _():
            place(scr, (index + 1) * ROWS, ROWS)

    @pl.when(part == 0)
    def _():
        place(gout_ref, 0, ROWS)

    @pl.when(part == 2)
    def _():
        bias = lax.dot_general(
            sums[...],
            order_ref[...].astype(f32),
            (((1,), (1,)), ((), ())),
            precision=lax.Precision.HIGHEST,
            preferred_element_type=f32,
        )
        rows = (
            bias[0:1], bias[2:3], one_ref[2:3, :], one_ref[0:1, :],
            one_ref[1:2, :], two_ref[2:3, :], two_ref[0:1, :], two_ref[1:2, :],
        )
        small[...] = jnp.zeros_like(small)
        for group in range(GROUPS_W):
            row, column = divmod(group, GROUPS_W // 8)
            small[group, 0:1, :N_VEC] = rows[row][:, column * N_VEC : (column + 1) * N_VEC]
            row, column = divmod(group, GROUPS_W // 4)
            small[group, 0:1, N_VEC : N_VEC + N_BIAS] = upb_ref[row, :, column * N_BIAS : (column + 1) * N_BIAS]
        place(small, 4 * ROWS, 8)


def grad_project(me, x, xp, grads, grad_out, sums_one, sums_two, up_bias, order):
    rows = x.shape[0]
    half = (GROUPS_W // 2, LAST_ROWS, D)
    return call(
        grad_project_body,
        (3,),
        [
            whole((rows, D)),
            whole((rows, D)),
            pl.BlockSpec((1, rows, D), lambda s, *_: (s, 0, 0)),
            whole((GROUPS_W, ROWS, D)),
            whole((8, D)),
            whole((8, D)),
            whole((FF // D, 1, D)),
            whole((D, D)),
        ],
        [whole(half)] * 2,
        [sds(half, bf16)] * 2,
        scratch=[
            pltpu.VMEM((GROUPS_W, ROWS, D), bf16),
            pltpu.VMEM((8, D), f32),
            pltpu.VMEM((GROUPS_W, 8, D), f32),
        ],
        prefetch=1,
        flops=6 * rows * D * D,
        moved=10 * rows * D + 12 * D * D,
        name="grad_project",
    )(me, x, xp, grads, grad_out, sums_one, sums_two, up_bias, order)


def grad_input_body(gres_ref, grads_ref, back_ref, w_ref, out_ref):
    total = gres_ref[...] + dot_nt(grads_ref[0], w_ref[0])
    for part in (1, 2):
        total = total + dot_nt(back_ref[part - 1], w_ref[part, :, :HALF])
        total = total + dot_nt(grads_ref[part, :, HALF:], w_ref[part, :, HALF:])
    out_ref[...] = total


def grad_input_of(gres, grads, back, weights):
    rows = gres.shape[0]
    step = 256
    row_spec = pl.BlockSpec((step, D), lambda i: (i, 0))
    return call(
        grad_input_body,
        (rows // step,),
        [
            row_spec,
            pl.BlockSpec((3, step, D), lambda i: (0, i, 0)),
            pl.BlockSpec((2, step, HALF), lambda i: (0, i, 0)),
            whole((3, D, D)),
        ],
        row_spec,
        sds((rows, D), f32),
        flops=6 * rows * D * D,
        moved=16 * rows * D + 6 * D * D,
        name="grad_input",
    )(gres, grads, back, weights)


def gather(value):
    return lax.all_gather(value, BOTH, axis=0)


def scatter(value):
    return lax.psum_scatter(value, BOTH, scatter_dimension=0)


def joined(gathered, start, rows, columns=1):
    count = gathered.shape[0]
    part = gathered[:, start : start + columns * rows]
    if columns > 1:
        part = part.reshape(GROUPS_W, count // GROUPS_W, columns, rows, D).transpose(0, 2, 1, 3, 4)
    return part.reshape(GROUPS_W, -1, D)


def parted(grouped, count, rows, columns=1):
    if columns > 1:
        grouped = grouped.reshape(GROUPS_W, columns, count // GROUPS_W, rows, D).transpose(0, 2, 1, 3, 4)
    return grouped.reshape(count, columns * rows, D)


def gather_near(shard):
    rows = shard.shape[0]
    half = rows // 16 * 8
    column = jnp.stack([shard] + [swap(shard, "dp", 2 * step) for step in range(1, 4)])
    over_x = swap(column, "dp", 1)
    over_y = swap(column, "blk", 2)
    over_both = jnp.concatenate((swap(over_y[:, :half], "dp", 1), swap(over_x[:, half:], "blk", 2)), axis=1)
    near = {(0, 0): column, (0, 1): over_x, (1, 0): over_y, (1, 1): over_both}
    pieces = {(0, y, x): value for (y, x), value in near.items()}
    pieces.update({(1, y, x): swap(value, "blk", 1) for (y, x), value in near.items()})
    return [pieces[key] for key in PIECES]


def over_cores(keep, send):
    rows = keep.shape[1]
    return (keep + swap(send, "blk", 1)).reshape(2, 4, 2, rows, D)


def over_first(total):
    rows = total.shape[3]
    half = (rows + 8) // 16 * 8
    one, two = total[:, :, :, :half], total[:, :, :, half:]
    return one[:, :, 0] + swap(one[:, :, 1], "dp", 1), two[0] + swap(two[1], "blk", 2)


def over_second(pair):
    one, two = pair
    one = one[0] + swap(one[1], "blk", 2)
    two = two[:, 0] + swap(two[:, 1], "dp", 1)
    return jnp.concatenate((one, two), axis=1)


def over_z(column):
    result = column[0].astype(f32)
    for step in range(1, 4):
        result = result + swap(column[step], "dp", 2 * step).astype(f32)
    return result


def together(*values):
    return lax.optimization_barrier(values)


def every_group(keep, send):
    rows = keep.shape[1]
    return jnp.stack((keep.reshape(2, 8, rows, D), send.reshape(2, 8, rows, D)), axis=1).reshape(GROUPS_W, rows, D)


def body(tokens, cotangent, lengths, head_mode, w_query, w_key, w_value, w_out, w_up, w_down, b_up, vectors):
    seq_count = tokens.shape[0]
    row_count = seq_count * BLOCK
    devices = lax.axis_size("blk") * lax.axis_size("dp")
    near = devices == GROUPS_W
    own_rows = D // devices
    n_vec, n_bias = vectors.shape[0], b_up.shape[0]
    blk_index = lax.axis_index("blk")
    device = blk_index * lax.axis_size("dp") + lax.axis_index("dp")
    me = (device if near else device * 0).reshape(1).astype(jnp.int32)
    block_side = blk_index % 2
    member = blk_index // 2
    seq_lengths = jnp.where(member == 0, lengths[:, 0], lengths[:, 1])
    valid = jnp.stack(
        (
            jnp.clip(seq_lengths - (1 - block_side) * BLOCK, 0, BLOCK),
            jnp.clip(seq_lengths - block_side * BLOCK, 0, BLOCK),
        ),
        axis=1,
    ).astype(jnp.int32)
    swapped = head_mode == 1
    place = jnp.where(swapped, jnp.cumsum(swapped) - 1, H // 2 + jnp.cumsum(~swapped) - 1)
    target = jnp.repeat(place * HD, HD) + jnp.tile(jnp.arange(HD), H)
    order = (target[:, None] == jnp.arange(D)[None, :]).astype(bf16)

    inputs = tokens.reshape(row_count, D)
    other_inputs = swap(inputs, "blk", 1)

    up_bias = lax.dynamic_update_slice(jnp.zeros((FF,), bf16), b_up, (device * n_bias,)).reshape(FF // D, D)
    ffn_shard = jnp.concatenate(
        (
            w_down.reshape(4 * own_rows, D),
            w_up.reshape(own_rows, 4, D).transpose(1, 0, 2).reshape(4 * own_rows, D),
            w_out.reshape(own_rows, D),
            jnp.pad(up_bias, ((0, 8 - FF // D), (0, 0))),
        )
    )
    ffn_pack = gather(ffn_shard)
    small = lax.dynamic_update_slice(jnp.zeros((8 * D,), bf16), vectors, (device * n_vec,)).reshape(8, D)
    stacked = jnp.concatenate([w.reshape(own_rows, D) for w in (w_query, w_key, w_value)] + [small[0:2]])
    stacked = dot_nn(stacked, order).astype(bf16)
    attn_shard = jnp.concatenate((stacked, small[2:]))
    if near:
        pieces = gather_near(attn_shard)
    else:
        attn_all = gather(attn_shard)
        attn_pack = jnp.concatenate(
            [joined(attn_all, s * own_rows, own_rows) for s in range(3)]
            + [jnp.sum(attn_all[:, 3 * own_rows :].reshape(GROUPS_W, -1, 8, D), axis=1)],
            axis=1,
        ).reshape(2, 2, 4, 2, 3 * ROWS + 8, D)
        pieces = [attn_pack[y, core, :, x] for core, y, x in PIECES]
        ffn_pack = jnp.concatenate(
            (
                joined(ffn_pack, 0, 4 * own_rows),
                joined(ffn_pack, 4 * own_rows, own_rows, 4),
                joined(ffn_pack, 8 * own_rows, own_rows),
                jnp.sum(ffn_pack[:, 9 * own_rows :].reshape(GROUPS_W, -1, 8, D), axis=1),
            ),
            axis=1,
        )

    q, k, v, attn_weights, vecs = project(me, inputs, other_inputs, pieces)
    ctx, probs = attend(valid, q, k, v)
    hat, inv, low, out_weight, up_biases = first_norm(ctx, inputs, ffn_pack, order, vecs)
    act, slope, output, gtwo, gsec, sums_two = ffn_forward(
        low, hat, cotangent.reshape(row_count, D), ffn_pack, up_biases, vecs
    )
    grad_down, gsec = together(grad_down_of(act, gsec), gsec)
    down_sum = scatter(parted(grad_down, devices, 4 * own_rows)).astype(f32)
    up_keep, up_send, grad_up_bias, acc = ffn_backward(me, gsec, slope, low, ffn_pack)
    gres, grad_ctx, grad_out, delta, sums_one = first_back(acc, gtwo, hat, inv, ctx, out_weight, order, vecs)
    if near:
        up_total, grad_ctx = together(over_cores(up_keep, up_send), grad_ctx)
    grads, give = attend_back(q, k, v, probs, grad_ctx, delta)
    if near:
        up_pair, grads = together(over_first(up_total), grads)
    back = swap(give, "blk", 1)
    last_keep, last_send = grad_project(
        me, inputs, other_inputs, grads, grad_out, sums_one, sums_two, grad_up_bias, order
    )
    if near:
        up_column = over_second(up_pair)
        last_total, up_column, gres = together(over_cores(last_keep, last_send), up_column, gres)
    grad_inputs = grad_input_of(gres, grads, back, attn_weights)

    if near:
        up_sum = over_z(up_column)
        last_sum = over_z(over_second(over_first(last_total)))
    else:
        up_sum = scatter(parted(every_group(up_keep, up_send), devices, own_rows, 4)).astype(f32)
        last = every_group(last_keep, last_send)
        tail = jnp.concatenate(
            (
                last[:, 4 * ROWS, :N_VEC].reshape(devices, n_vec),
                last[:, 4 * ROWS, N_VEC : N_VEC + N_BIAS].reshape(devices, n_bias),
            ),
            axis=1,
        )
        tail = jnp.pad(tail, ((0, 0), (0, D - n_vec - n_bias)))[:, None, :]
        last_sum = scatter(
            jnp.concatenate(
                [parted(last[:, s * ROWS : (s + 1) * ROWS], devices, own_rows) for s in range(4)] + [tail], axis=1
            )
        ).astype(f32)
    qkv_sum = lax.dot_general(
        last_sum[own_rows : 4 * own_rows],
        order.astype(f32),
        (((1,), (1,)), ((), ())),
        precision=lax.Precision.HIGHEST,
    ).reshape(3, own_rows * D)
    small_sum = last_sum[4 * own_rows]
    return (
        output.reshape(tokens.shape),
        grad_inputs.reshape(tokens.shape),
        qkv_sum[0],
        qkv_sum[1],
        qkv_sum[2],
        last_sum[:own_rows].reshape(-1),
        up_sum.reshape(4, own_rows, D).transpose(1, 0, 2).reshape(-1),
        down_sum.reshape(-1),
        small_sum[n_vec : n_vec + n_bias],
        small_sum[:n_vec],
    )


def solution(mesh):
    flat = P(BOTH)
    block = P("dp", "blk", None, None)
    return jax.shard_map(
        body,
        mesh=mesh,
        in_specs=(block, block, P("dp", None), P(), *([flat] * 8)),
        out_specs=(block, block, *([flat] * 8)),
        check_vma=False,
    )
```

```python
from functools import partial

import jax
import jax.numpy as jnp
from jax import lax
from jax.experimental import pallas as pl
from jax.experimental.pallas import tpu as pltpu
from jax.sharding import PartitionSpec as P

D = 768
H = 12
HD = 64
FF = 3072
BLOCK = 512
HALF = D // 2
PAIR = 2 * HD
LANES = 128
GROUPS_W = 32
ROWS = D // GROUPS_W

norm_eps = 1e-05
masked_fill = -1000000000.0
LOG2E = 1.4426950408889634
SQRT_HALF = 0.7071067811865476
INV_SQRT_2PI = 0.3989422804014327

bf16 = jnp.bfloat16
f32 = jnp.float32
BOTH = ("blk", "dp")


def swap(value, axis, mask):
    return lax.ppermute(value, axis, [(source, source ^ mask) for source in range(lax.axis_size(axis))])


def dot_nn(a, b):
    return lax.dot_general(a, b, (((1,), (0,)), ((), ())), preferred_element_type=f32)


def dot_nt(a, b):
    return lax.dot_general(a, b, (((1,), (1,)), ((), ())), preferred_element_type=f32)


def dot_tn(a, b):
    return lax.dot_general(a, b, (((0,), (0,)), ((), ())), preferred_element_type=f32)


def whole(shape):
    return pl.BlockSpec(shape, lambda *_: (0,) * len(shape))


def call(body, grid, in_specs, out_specs, out_shape, scratch=(), prefetch=0, flops=0, moved=0, name=None):
    return pl.pallas_call(
        body,
        grid_spec=pltpu.PrefetchScalarGridSpec(
            num_scalar_prefetch=prefetch,
            grid=grid,
            in_specs=in_specs,
            out_specs=out_specs,
            scratch_shapes=list(scratch),
        ),
        out_shape=out_shape,
        compiler_params=pltpu.CompilerParams(vmem_limit_bytes=60 * 1024 * 1024),
        cost_estimate=pl.CostEstimate(flops=flops, bytes_accessed=moved, transcendentals=0),
        name=name,
    )


def sds(shape, dtype):
    return jax.ShapeDtypeStruct(shape, dtype)


def square(ref):
    return ref[...].reshape(D, D)


PIECES = [(core, y, x) for core in range(2) for y in range(2) for x in range(2)]


def project_body(me_ref, x_ref, xp_ref, *refs):
    pieces, (order_ref, q_ref, k_ref, v_ref, w_ref, out_ref, vec_ref, upb_ref, scr) = refs[: len(PIECES)], refs[len(PIECES) :]

    @pl.when(pl.program_id(0) == 0)
    def _():
        me = me_ref[0]
        total = jnp.zeros((8, D), f32)
        up_bias = jnp.zeros((8, D), f32)
        for (core, y, x), piece in zip(PIECES, pieces):
            for z in range(piece.shape[0]):
                group = (16 * y + 8 * core + 2 * z + x) ^ me
                for part in range(4):
                    scr[part, group] = piece[z, part * ROWS : (part + 1) * ROWS, :]
                total = total + piece[z, 4 * ROWS : 4 * ROWS + 8, :].astype(f32)
                up_bias = up_bias + piece[z, 4 * ROWS + 8 : 4 * ROWS + 16, :].astype(f32)
        vec_ref[...] = total
        upb_ref[...] = up_bias
        for part in range(3):
            w_ref[part] = scr[part].reshape(D, D)
        out_ref[...] = dot_tn(order_ref[...], scr[3].reshape(D, D)).astype(bf16)

    own, other = x_ref[...], xp_ref[...]
    q_ref[...] = (dot_nn(own, w_ref[0]) + vec_ref[0:1, :]).astype(bf16)
    k_ref[:, :HALF] = dot_nn(other, w_ref[1, :, :HALF]).astype(bf16)
    k_ref[:, HALF:] = dot_nn(own, w_ref[1, :, HALF:]).astype(bf16)
    v_ref[:, :HALF] = (dot_nn(other, w_ref[2, :, :HALF]) + vec_ref[1:2, :HALF]).astype(bf16)
    v_ref[:, HALF:] = (dot_nn(own, w_ref[2, :, HALF:]) + vec_ref[1:2, HALF:]).astype(bf16)


def project(me, x, xp, pieces, order):
    rows = x.shape[0]
    step = BLOCK
    row_spec = pl.BlockSpec((step, D), lambda i, *_: (i, 0))
    return call(
        project_body,
        (rows // step,),
        [row_spec, row_spec] + [whole(pieces[0].shape)] * len(PIECES) + [whole((D, D))],
        [row_spec] * 3 + [whole((3, D, D)), whole((D, D)), whole((8, D)), whole((8, D))],
        [sds((rows, D), bf16)] * 3 + [sds((3, D, D), bf16), sds((D, D), bf16), sds((8, D), f32), sds((8, D), f32)],
        scratch=[pltpu.VMEM((4, GROUPS_W, ROWS, D), bf16)],
        prefetch=1,
        flops=6 * rows * D * D,
        moved=10 * rows * D + 12 * D * D,
        name="project",
    )(me, x, xp, *pieces, order)


def attend_body(valid_ref, q_ref, k_ref, v_ref, ctx_ref, p_ref):
    seq, pair = pl.program_id(0), pl.program_id(1)
    valid = valid_ref[seq, pair // 3]
    queries, keys, values = q_ref[...], k_ref[...], v_ref[...]
    lane = lax.broadcasted_iota(jnp.int32, (BLOCK, PAIR), 1)
    key_row = lax.broadcasted_iota(jnp.int32, (BLOCK, 1), 0)
    fill = jnp.where(key_row < valid, 0.0, masked_fill * LOG2E)
    parts = []
    for head in range(2):
        mine = (lane < HD) if head == 0 else (lane >= HD)
        masked = jnp.where(mine, queries, jnp.zeros_like(queries))
        scores = dot_nt(keys, masked) * (LOG2E * HD ** (-0.5)) + fill
        top = jnp.max(scores, axis=0, keepdims=True)
        weights = jnp.exp2(scores - top)
        total = jnp.sum(weights, axis=0, keepdims=True)
        probs = (weights * (1.0 / total)).astype(bf16)
        p_ref[0, head] = probs
        parts.append(dot_tn(probs, values))
    ctx_ref[...] = jnp.where(lane < HD, parts[0], parts[1]).astype(bf16)


def attend(valid, q, k, v):
    rows = q.shape[0]
    seqs = rows // BLOCK
    spec = pl.BlockSpec((BLOCK, PAIR), lambda s, j, *_: (s, j))
    return call(
        attend_body,
        (seqs, H // 2),
        [spec] * 3,
        [spec, pl.BlockSpec((1, 2, BLOCK, BLOCK), lambda s, j, *_: (s, j, 0, 0))],
        [sds((rows, D), bf16), sds((seqs, H, BLOCK, BLOCK), bf16)],
        prefetch=1,
        flops=16 * rows * BLOCK * D,
        moved=8 * rows * D + 2 * rows * H * BLOCK,
        name="attend",
    )(valid, q, k, v)


def attend_back_body(q_ref, k_ref, v_ref, p_ref, gctx_ref, out_ref, give_ref):
    pair = pl.program_id(1)
    queries, keys, values, grad_ctx = q_ref[...], k_ref[...], v_ref[...], gctx_ref[...]
    lane = lax.broadcasted_iota(jnp.int32, (BLOCK, PAIR), 1)
    scale = HD ** (-0.5)
    gq, gk, gv = [], [], []
    for head in range(2):
        mine = (lane < HD) if head == 0 else (lane >= HD)
        probs = p_ref[0, head]
        grad_probs = dot_nt(jnp.where(mine, values, jnp.zeros_like(values)), grad_ctx)
        delta = jnp.sum(probs.astype(f32) * grad_probs, axis=0, keepdims=True)
        grad_scores = (probs.astype(f32) * (grad_probs - delta)).astype(bf16)
        gv.append(dot_nn(probs, grad_ctx))
        gk.append(dot_nn(grad_scores, queries))
        gq.append(dot_tn(grad_scores, keys))
    first = lane < HD
    out_ref[0] = (jnp.where(first, gq[0], gq[1]) * scale).astype(bf16)
    grad_keys = (jnp.where(first, gk[0], gk[1]) * scale).astype(bf16)
    grad_values = jnp.where(first, gv[0], gv[1]).astype(bf16)
    out_ref[1] = grad_keys
    out_ref[2] = grad_values

    @pl.when(pair < H // 4)
    def _():
        give_ref[0] = grad_keys
        give_ref[1] = grad_values


def attend_back(q, k, v, probs, grad_ctx):
    rows = q.shape[0]
    seqs = rows // BLOCK
    spec = pl.BlockSpec((BLOCK, PAIR), lambda s, j: (s, j))
    return call(
        attend_back_body,
        (seqs, H // 2),
        [spec] * 3
        + [
            pl.BlockSpec((1, 2, BLOCK, BLOCK), lambda s, j: (s, j, 0, 0)),
            spec,
        ],
        [
            pl.BlockSpec((3, BLOCK, PAIR), lambda s, j: (0, s, j)),
            pl.BlockSpec((2, BLOCK, PAIR), lambda s, j: (0, s, jnp.minimum(j, H // 4 - 1))),
        ],
        [sds((3, rows, D), bf16), sds((2, rows, HALF), bf16)],
        flops=32 * rows * BLOCK * D,
        moved=14 * rows * D + 2 * rows * H * BLOCK,
        name="attend_back",
    )(q, k, v, probs, grad_ctx)


def mean_last(value):
    return jnp.sum(value, axis=-1, keepdims=True) * (1.0 / D)


def first_norm_body(ctx_ref, x_ref, wop_ref, vec_ref, hat_ref, inv_ref, low_ref):
    branch = dot_nn(ctx_ref[...], wop_ref[...]) + vec_ref[2:3, :]
    residual = x_ref[...].astype(f32) + branch
    centred = residual - mean_last(residual)
    inv = lax.rsqrt(mean_last(centred * centred) + norm_eps)
    hat = centred * inv
    hat_ref[...] = hat
    inv_ref[...] = jnp.broadcast_to(inv, inv_ref.shape)
    low_ref[...] = (hat * vec_ref[3:4, :] + vec_ref[4:5, :]).astype(bf16)


def first_norm(ctx, x, wop, vecs):
    rows = x.shape[0]
    step = BLOCK
    row_spec = pl.BlockSpec((step, D), lambda i: (i, 0))
    return call(
        first_norm_body,
        (rows // step,),
        [row_spec, row_spec, whole((D, D)), whole((8, D))],
        [row_spec, pl.BlockSpec((step, LANES), lambda i: (i, 0)), row_spec],
        [sds((rows, D), f32), sds((rows, LANES), f32), sds((rows, D), bf16)],
        flops=2 * rows * D * D,
        moved=12 * rows * D,
        name="first_norm",
    )(ctx, x, wop, vecs)


def gelu_and_slope(value):
    size = jnp.abs(value)
    gauss = jnp.exp2(value * value * (-0.5 * LOG2E))
    knot = 1.0 / (1.0 + size * (0.3275911 * SQRT_HALF))
    poly = knot * (
        0.254829592 + knot * (-0.284496736 + knot * (1.421413741 + knot * (-1.453152027 + knot * 1.061405429)))
    )
    tail = 0.5 * poly * gauss
    normal_cdf = jnp.where(value >= 0.0, 1.0 - tail, tail)
    return value * normal_cdf, normal_cdf + value * gauss * INV_SQRT_2PI


def ffn_forward_body(
    low_ref, hat_ref, cot_ref, up_ref, down_ref, bias_ref, vec_ref,
    act_ref, slope_ref, out_ref, gtwo_ref, gsec_ref, sums_ref, acc,
):
    chunk, last = pl.program_id(1), pl.num_programs(1) - 1
    first = (pl.program_id(0) == 0) & (chunk == 0)
    rows = low_ref.shape[0]
    step = 256
    w_up = square(up_ref)
    w_down = square(down_ref)

    @pl.when(first)
    def _():
        sums_ref[...] = jnp.zeros_like(sums_ref)

    @pl.when(chunk == 0)
    def _():
        acc[...] = jnp.zeros_like(acc)

    for start in range(0, rows, step):
        part = pl.ds(start, step)
        hidden = dot_nn(low_ref[part, :], w_up) + bias_ref[pl.ds(chunk, 1), :]
        activated, slope = gelu_and_slope(hidden)
        activated = activated.astype(bf16)
        act_ref[part, :] = activated
        slope_ref[part, :] = slope.astype(bf16)
        down = dot_nn(activated, w_down)

        acc[part, :] += down

    @pl.when(chunk == last)
    def _():
        gain, bias = vec_ref[6:7, :], vec_ref[7:8, :]

        def rows_of(index, sums):
            part = pl.ds(pl.multiple_of(index * step, step), step)
            residual = hat_ref[part, :] * vec_ref[3:4, :] + vec_ref[4:5, :] + (acc[part, :] + vec_ref[5:6, :])
            centred = residual - mean_last(residual)
            inv = lax.rsqrt(mean_last(centred * centred) + norm_eps)
            hat = centred * inv
            out_ref[part, :] = (hat * gain + bias).astype(bf16)
            cot = cot_ref[part, :].astype(f32)
            scaled = cot * gain
            grad = inv * (scaled - mean_last(scaled) - hat * mean_last(scaled * hat))
            gtwo_ref[part, :] = grad
            low = grad.astype(bf16)
            gsec_ref[part, :] = low
            return (
                sums[0] + jnp.sum(cot * hat, axis=0, keepdims=True),
                sums[1] + jnp.sum(cot, axis=0, keepdims=True),
                sums[2] + jnp.sum(low.astype(f32), axis=0, keepdims=True),
            )

        zero = jnp.zeros((1, D), f32)
        sums = lax.fori_loop(0, rows // step, rows_of, (zero, zero, zero))
        for index, value in enumerate(sums):
            sums_ref[index : index + 1, :] += value


def ffn_forward(low, hat, cot, pack, up_bias, vecs):
    rows = low.shape[0]
    span = 1024
    chunks = FF // D
    row_spec = pl.BlockSpec((span, D), lambda r, c: (r, 0))
    wide = pl.BlockSpec((span, D), lambda r, c: (r, c))
    return call(
        ffn_forward_body,
        (rows // span, chunks),
        [
            row_spec,
            row_spec,
            row_spec,
            pl.BlockSpec((GROUPS_W, ROWS, D), lambda r, c: (0, 4 + c, 0)),
            pl.BlockSpec((GROUPS_W // 4, 4 * ROWS, D), lambda r, c: (c, 0, 0)),
            whole((8, D)),
            whole((8, D)),
        ],
        [wide, wide, row_spec, row_spec, row_spec, whole((8, D))],
        [
            sds((rows, FF), bf16),
            sds((rows, FF), bf16),
            sds((rows, D), bf16),
            sds((rows, D), f32),
            sds((rows, D), bf16),
            sds((8, D), f32),
        ],
        scratch=[pltpu.VMEM((span, D), f32)],
        flops=4 * rows * D * FF,
        moved=26 * rows * D + 4 * D * FF,
        name="ffn_forward",
    )(low, hat, cot, pack, pack, up_bias, vecs)


def grad_down_body(me_ref, act_ref, gsec_ref, keep_ref, send_ref, scr):
    step = pl.program_id(0)
    scr[...] = dot_tn(act_ref[...], gsec_ref[...]).astype(bf16).reshape(scr.shape)
    place = jnp.bitwise_and(me_ref[0], 7)

    @pl.when(step < 2)
    def _():
        for index in range(8):
            keep_ref[0, index] = scr[place ^ index]

    @pl.when(step >= 2)
    def _():
        for index in range(8):
            send_ref[0, index] = scr[place ^ index]


def grad_down_of(me, act, gsec):
    rows = act.shape[0]
    block = (1, GROUPS_W // 4, 4 * ROWS, D)
    return call(
        grad_down_body,
        (FF // D,),
        [
            pl.BlockSpec((rows, D), lambda s, me_ref: (0, ((s % 2) * 2 + s // 2) ^ (me_ref[0] // 8))),
            whole((rows, D)),
        ],
        [
            pl.BlockSpec(block, lambda s, me_ref: (jnp.minimum(s, 1), 0, 0, 0)),
            pl.BlockSpec(block, lambda s, me_ref: (jnp.maximum(s - 2, 0), 0, 0, 0)),
        ],
        [sds((2, *block[1:]), bf16)] * 2,
        scratch=[pltpu.VMEM(block[1:], bf16)],
        prefetch=1,
        flops=2 * rows * D * FF,
        moved=10 * rows * D + 2 * D * FF,
        name="grad_down",
    )(me, act, gsec)


def apart(scr, me, keep, send):
    def one(index, carry):
        group = (2 * index - jnp.bitwise_and(index, 7)) ^ me
        keep(index, scr[group])
        send(index, scr[group ^ 8])
        return carry

    lax.fori_loop(0, GROUPS_W // 2, one, 0)


def ffn_backward_body(
    me_ref, gsec_ref, slope_ref, low_ref, up_ref, down_ref, keep_ref, send_ref, gbias_ref, acc_ref, scr
):
    chunk = pl.program_id(0)
    grad_act = dot_nt(gsec_ref[...], square(down_ref))
    grad_hidden = (grad_act * slope_ref[...].astype(f32)).astype(bf16)
    gbias_ref[0] = jnp.sum(grad_hidden.astype(f32), axis=0, keepdims=True)
    scr[...] = dot_tn(low_ref[...], grad_hidden).astype(bf16).reshape(scr.shape)

    def keep(index, value):
        keep_ref[index] = value

    def send(index, value):
        send_ref[index] = value

    apart(scr, me_ref[0], keep, send)
    back = dot_nt(grad_hidden, square(up_ref))

    @pl.when(chunk == 0)
    def _():
        acc_ref[...] = back

    @pl.when(chunk > 0)
    def _():
        acc_ref[...] += back


def ffn_backward(me, gsec, slope, low, pack):
    rows = gsec.shape[0]
    half = pl.BlockSpec((GROUPS_W // 2, ROWS, D), lambda c, *_: (0, c, 0))
    return call(
        ffn_backward_body,
        (FF // D,),
        [
            whole((rows, D)),
            pl.BlockSpec((rows, D), lambda c, *_: (0, c)),
            whole((rows, D)),
            pl.BlockSpec((GROUPS_W, ROWS, D), lambda c, *_: (0, 4 + c, 0)),
            pl.BlockSpec((GROUPS_W // 4, 4 * ROWS, D), lambda c, *_: (c, 0, 0)),
        ],
        [half, half, pl.BlockSpec((1, 1, D), lambda c, *_: (c, 0, 0)), whole((rows, D))],
        [sds((GROUPS_W // 2, 4 * ROWS, D), bf16)] * 2 + [sds((FF // D, 1, D), f32), sds((rows, D), f32)],
        scratch=[pltpu.VMEM((GROUPS_W, ROWS, D), bf16)],
        prefetch=1,
        flops=6 * rows * D * FF,
        moved=16 * rows * D + 6 * D * FF,
        name="ffn_backward",
    )(me, gsec, slope, low, pack, pack)


def first_back_body(
    acc_ref, gtwo_ref, hat_ref, inv_ref, ctx_ref, wop_ref, order_ref, vec_ref,
    gres_ref, gctx_ref, gout_ref, sums_ref, gout_scr,
):
    index, last = pl.program_id(0), pl.num_programs(0) - 1
    hat = hat_ref[...]
    inv = inv_ref[:, 0:1]
    grad_first = gtwo_ref[...] + acc_ref[...]
    scaled = grad_first * vec_ref[3:4, :]
    grad = inv * (scaled - mean_last(scaled) - hat * mean_last(scaled * hat))
    gres_ref[...] = grad
    low = grad.astype(bf16)
    ctx = ctx_ref[...]
    gctx_ref[...] = dot_nt(low, wop_ref[...]).astype(bf16)
    grad_out = dot_tn(ctx, low)

    @pl.when(index == 0)
    def _():
        gout_scr[...] = grad_out
        sums_ref[...] = jnp.zeros_like(sums_ref)

    @pl.when(index > 0)
    def _():
        gout_scr[...] += grad_out

    sums_ref[0:1, :] += jnp.sum(grad_first * hat, axis=0, keepdims=True)
    sums_ref[1:2, :] += jnp.sum(grad_first, axis=0, keepdims=True)
    sums_ref[2:3, :] += jnp.sum(low.astype(f32), axis=0, keepdims=True)

    @pl.when(index == last)
    def _():
        ordered = dot_nn(order_ref[...], gout_scr[...].astype(bf16))
        gout_ref[...] = ordered.astype(bf16).reshape(gout_ref.shape)


def first_back(acc, gtwo, hat, inv, ctx, wop, order, vecs):
    rows = acc.shape[0]
    step = 256
    row_spec = pl.BlockSpec((step, D), lambda i: (i, 0))
    return call(
        first_back_body,
        (rows // step,),
        [
            row_spec,
            row_spec,
            row_spec,
            pl.BlockSpec((step, LANES), lambda i: (i, 0)),
            row_spec,
            whole((D, D)),
            whole((D, D)),
            whole((8, D)),
        ],
        [
            row_spec,
            row_spec,
            whole((GROUPS_W, ROWS, D)),
            whole((8, D)),
        ],
        [
            sds((rows, D), f32),
            sds((rows, D), bf16),
            sds((GROUPS_W, ROWS, D), bf16),
            sds((8, D), f32),
        ],
        scratch=[pltpu.VMEM((D, D), f32)],
        flops=4 * rows * D * D,
        moved=20 * rows * D + 6 * D * D,
        name="first_back",
    )(acc, gtwo, hat, inv, ctx, wop, order, vecs)


def in_order(rows, order):
    high = rows.astype(bf16)
    rest = rows - high.astype(f32)
    middle = rest.astype(bf16)
    low = (rest - middle.astype(f32)).astype(bf16)
    return dot_nt(high, order) + (dot_nt(middle, order) + dot_nt(low, order))


LAST_ROWS = 4 * ROWS + 8
N_VEC = 8 * D // GROUPS_W
N_BIAS = FF // GROUPS_W


def grad_project_body(
    me_ref, x_ref, xp_ref, grad_ref, gout_ref, one_ref, two_ref, upb_ref, order_ref, keep_ref, send_ref, scr, sums, small
):
    part = pl.program_id(0)
    me = me_ref[0]
    own = x_ref[...]
    other = jnp.where(part == 0, own, xp_ref[...])
    grad = grad_ref[0]
    left = dot_tn(other, grad[:, :HALF]).astype(bf16)
    right = dot_tn(own, grad[:, HALF:]).astype(bf16)
    scr[:, :, :HALF] = left.reshape(GROUPS_W, ROWS, HALF)
    scr[:, :, HALF:] = right.reshape(GROUPS_W, ROWS, HALF)
    sums[pl.ds(part, 1), :] = jnp.sum(grad.astype(f32), axis=0, keepdims=True)

    def place(source, start, size):
        def keep(index, value):
            keep_ref[index, start : start + size, :] = value.astype(bf16)

        def send(index, value):
            send_ref[index, start : start + size, :] = value.astype(bf16)

        apart(source, me, keep, send)

    for index in range(3):

        @pl.when(part == index)
        def _():
            place(scr, (index + 1) * ROWS, ROWS)

    @pl.when(part == 0)
    def _():
        place(gout_ref, 0, ROWS)

    @pl.when(part == 2)
    def _():
        bias = in_order(sums[...], order_ref[...])
        rows = (
            bias[0:1], bias[2:3], one_ref[2:3, :], one_ref[0:1, :],
            one_ref[1:2, :], two_ref[2:3, :], two_ref[0:1, :], two_ref[1:2, :],
        )
        small[...] = jnp.zeros_like(small)
        for group in range(GROUPS_W):
            row, column = divmod(group, GROUPS_W // 8)
            small[group, 0:1, :N_VEC] = rows[row][:, column * N_VEC : (column + 1) * N_VEC]
            row, column = divmod(group, GROUPS_W // 4)
            small[group, 0:1, N_VEC : N_VEC + N_BIAS] = upb_ref[row, :, column * N_BIAS : (column + 1) * N_BIAS]
        place(small, 4 * ROWS, 8)


def grad_project(me, x, xp, grads, grad_out, sums_one, sums_two, up_bias, order):
    rows = x.shape[0]
    half = (GROUPS_W // 2, LAST_ROWS, D)
    return call(
        grad_project_body,
        (3,),
        [
            whole((rows, D)),
            whole((rows, D)),
            pl.BlockSpec((1, rows, D), lambda s, *_: (s, 0, 0)),
            whole((GROUPS_W, ROWS, D)),
            whole((8, D)),
            whole((8, D)),
            whole((FF // D, 1, D)),
            whole((D, D)),
        ],
        [whole(half)] * 2,
        [sds(half, bf16)] * 2,
        scratch=[
            pltpu.VMEM((GROUPS_W, ROWS, D), bf16),
            pltpu.VMEM((8, D), f32),
            pltpu.VMEM((GROUPS_W, 8, D), f32),
        ],
        prefetch=1,
        flops=6 * rows * D * D,
        moved=10 * rows * D + 12 * D * D,
        name="grad_project",
    )(me, x, xp, grads, grad_out, sums_one, sums_two, up_bias, order)


def grad_input_body(gres_ref, grads_ref, back_ref, w_ref, out_ref):
    total = gres_ref[...] + dot_nt(grads_ref[0], w_ref[0])
    for part in (1, 2):
        total = total + dot_nt(back_ref[part - 1], w_ref[part, :, :HALF])
        total = total + dot_nt(grads_ref[part, :, HALF:], w_ref[part, :, HALF:])
    out_ref[...] = total


def grad_input_of(gres, grads, back, weights):
    rows = gres.shape[0]
    step = 256
    row_spec = pl.BlockSpec((step, D), lambda i: (i, 0))
    return call(
        grad_input_body,
        (rows // step,),
        [
            row_spec,
            pl.BlockSpec((3, step, D), lambda i: (0, i, 0)),
            pl.BlockSpec((2, step, HALF), lambda i: (0, i, 0)),
            whole((3, D, D)),
        ],
        row_spec,
        sds((rows, D), f32),
        flops=6 * rows * D * D,
        moved=16 * rows * D + 6 * D * D,
        name="grad_input",
    )(gres, grads, back, weights)


def summed(refs, start, stop):
    total = refs[0][start:stop, :].astype(f32)
    for ref in refs[1:]:
        total = total + ref[start:stop, :].astype(f32)
    return total


def spread(out_ref, total, first, stride):
    for column in range(D // LANES):
        out_ref[pl.ds(first + column, total.shape[0], stride=stride), :] = total[:, column * LANES : (column + 1) * LANES]


def finish_ffn_body(*refs):
    up_ref, down_ref = refs[6:]
    for chunk in range(4):
        spread(up_ref, summed(refs[:3], chunk * ROWS, (chunk + 1) * ROWS), chunk * (D // LANES), FF // LANES)
    spread(down_ref, summed(refs[3:6], 0, 4 * ROWS), 0, D // LANES)


def finish_last_body(*refs):
    order_ref, out_ref, q_ref, k_ref, v_ref, vec_ref, upb_ref = refs[6:]
    one, two = refs[:3], refs[3:6]
    half = one[0].shape[0]
    spread(out_ref, summed(one, 0, ROWS), 0, D // LANES)
    middle = jnp.concatenate((summed(one, ROWS, half), summed(two, 0, 4 * ROWS - half)), axis=0)
    ordered = in_order(middle, order_ref[...])
    for part, ref in enumerate((q_ref, k_ref, v_ref)):
        spread(ref, ordered[part * ROWS : (part + 1) * ROWS], 0, D // LANES)
    small = summed(two, 4 * ROWS - half, 4 * ROWS - half + 8)
    vec_ref[...] = small[0, :N_VEC]
    upb_ref[...] = small[0, N_VEC : N_VEC + N_BIAS]


def z_first(one, two):
    return swap(one[1:3], "dp", 2), swap(two[2:4], "dp", 6)


def z_second(one, two, got_one, got_two):
    return swap(one[3] + got_one[1], "dp", 6), swap(two[1] + got_two[0], "dp", 2)


def finish(body, one, two, got, last, extra, sizes, name):
    shapes = [(size * D // LANES, LANES) for size in sizes]
    if extra:
        shapes = shapes + [(N_VEC,), (N_BIAS,)]

    def piece(value, index):
        return pl.BlockSpec((None, *value.shape[1:]), lambda i: (index, 0, 0))

    return call(
        body,
        (1,),
        [piece(one, 0), piece(got[0], 0), whole(last[0].shape), piece(two, 0), piece(got[1], 1), whole(last[1].shape)]
        + [whole(value.shape) for value in extra],
        [whole(shape) for shape in shapes],
        [sds(shape, f32) for shape in shapes],
        moved=8 * (one.shape[1] + two.shape[1]) * D,
        name=name,
    )(one, got[0], last[0], two, got[1], last[1], *extra)


def gather(value):
    return lax.all_gather(value, BOTH, axis=0)


def scatter(value):
    return lax.psum_scatter(value, BOTH, scatter_dimension=0)


def joined(gathered, start, rows, columns=1):
    count = gathered.shape[0]
    part = gathered[:, start : start + columns * rows]
    if columns > 1:
        part = part.reshape(GROUPS_W, count // GROUPS_W, columns, rows, D).transpose(0, 2, 1, 3, 4)
    return part.reshape(GROUPS_W, -1, D)


def parted(grouped, count, rows, columns=1):
    if columns > 1:
        grouped = grouped.reshape(GROUPS_W, columns, count // GROUPS_W, rows, D).transpose(0, 2, 1, 3, 4)
    return grouped.reshape(count, columns * rows, D)


def gather_near(shard):
    rows = shard.shape[0]
    half = rows // 16 * 8
    column = jnp.stack([shard] + [swap(shard, "dp", 2 * step) for step in range(1, 4)])
    over_x = swap(column, "dp", 1)
    over_y = swap(column, "blk", 2)
    over_both = jnp.concatenate((swap(over_y[:, :half], "dp", 1), swap(over_x[:, half:], "blk", 2)), axis=1)
    near = {(0, 0): column, (0, 1): over_x, (1, 0): over_y, (1, 1): over_both}
    pieces = {(0, y, x): value for (y, x), value in near.items()}
    pieces.update({(1, y, x): swap(value, "blk", 1) for (y, x), value in near.items()})
    return [pieces[key] for key in PIECES]


def over_cores(keep, received):
    return (keep + received).reshape(2, 4, 2, keep.shape[1], D)


def over_x(total):
    return total[:, :, 0] + swap(total[:, :, 1], "dp", 1)


def over_y(total):
    return total[0] + swap(total[1], "blk", 2)


def over_first(total):
    rows = total.shape[3]
    half = (rows + 8) // 16 * 8
    one, two = total[:, :, :, :half], total[:, :, :, half:]
    return one[:, :, 0] + swap(one[:, :, 1], "dp", 1), two[0] + swap(two[1], "blk", 2)


def over_second(pair):
    one, two = pair
    one = one[0] + swap(one[1], "blk", 2)
    two = two[:, 0] + swap(two[:, 1], "dp", 1)
    return one, two


def together(*values):
    return lax.optimization_barrier(values)


def every_group(keep, send):
    rows = keep.shape[1]
    return jnp.stack((keep.reshape(2, 8, rows, D), send.reshape(2, 8, rows, D)), axis=1).reshape(GROUPS_W, rows, D)


def body(tokens, cotangent, lengths, head_mode, w_query, w_key, w_value, w_out, w_up, w_down, b_up, vectors):
    seq_count = tokens.shape[0]
    row_count = seq_count * BLOCK
    devices = lax.axis_size("blk") * lax.axis_size("dp")
    near = devices == GROUPS_W
    own_rows = D // devices
    n_vec, n_bias = vectors.shape[0], b_up.shape[0]
    blk_index = lax.axis_index("blk")
    device = blk_index * lax.axis_size("dp") + lax.axis_index("dp")
    me = (device if near else device * 0).reshape(1).astype(jnp.int32)
    block_side = blk_index % 2
    member = blk_index // 2
    seq_lengths = jnp.where(member == 0, lengths[:, 0], lengths[:, 1])
    valid = jnp.stack(
        (
            jnp.clip(seq_lengths - (1 - block_side) * BLOCK, 0, BLOCK),
            jnp.clip(seq_lengths - block_side * BLOCK, 0, BLOCK),
        ),
        axis=1,
    ).astype(jnp.int32)
    swapped = head_mode == 1
    place = jnp.where(swapped, jnp.cumsum(swapped) - 1, H // 2 + jnp.cumsum(~swapped) - 1)
    target = jnp.repeat(place * HD, HD) + jnp.tile(jnp.arange(HD), H)
    order = (target[:, None] == jnp.arange(D)[None, :]).astype(bf16)

    inputs = tokens.reshape(row_count, D)
    other_inputs = swap(inputs, "blk", 1)

    ffn_shard = jnp.concatenate(
        (
            w_down.reshape(4 * own_rows, D),
            w_up.reshape(own_rows, 4, D).transpose(1, 0, 2).reshape(4 * own_rows, D),
        )
    )
    ffn_pack = gather(ffn_shard)
    up_bias = lax.dynamic_update_slice(jnp.zeros((8 * D,), bf16), b_up, (device * n_bias,)).reshape(8, D)
    small = lax.dynamic_update_slice(jnp.zeros((8 * D,), bf16), vectors, (device * n_vec,)).reshape(8, D)
    stacked = jnp.concatenate([w.reshape(own_rows, D) for w in (w_query, w_key, w_value)] + [small[0:2]])
    stacked = dot_nn(stacked, order).astype(bf16)
    attn_shard = jnp.concatenate(
        (stacked[: 3 * own_rows], w_out.reshape(own_rows, D), stacked[3 * own_rows :], small[2:], up_bias)
    )
    if near:
        pieces = gather_near(attn_shard)
    else:
        attn_all = gather(attn_shard)
        attn_pack = jnp.concatenate(
            [joined(attn_all, s * own_rows, own_rows) for s in range(4)]
            + [jnp.sum(attn_all[:, 4 * own_rows :].reshape(GROUPS_W, -1, 16, D), axis=1)],
            axis=1,
        ).reshape(2, 2, 4, 2, 4 * ROWS + 16, D)
        pieces = [attn_pack[y, core, :, x] for core, y, x in PIECES]
        ffn_pack = jnp.concatenate(
            (joined(ffn_pack, 0, 4 * own_rows), joined(ffn_pack, 4 * own_rows, own_rows, 4)), axis=1
        )

    q, k, v, attn_weights, out_weight, vecs, up_biases = project(me, inputs, other_inputs, pieces, order)
    ctx, probs = attend(valid, q, k, v)
    hat, inv, low = first_norm(ctx, inputs, out_weight, vecs)
    act, slope, output, gtwo, gsec, sums_two = ffn_forward(
        low, hat, cotangent.reshape(row_count, D), ffn_pack, up_biases, vecs
    )
    down_keep, down_send = grad_down_of(me, act, gsec)
    down_keep, down_send = (value.reshape(GROUPS_W // 2, 4 * ROWS, D) for value in (down_keep, down_send))
    down_keep, down_send, gsec = together(down_keep, down_send, gsec)
    up_keep, up_send, grad_up_bias, acc = ffn_backward(me, gsec, slope, low, ffn_pack)
    if near:
        received, acc = together(swap(down_send, "blk", 1), acc)
        down = over_cores(down_keep, received)
    gres, grad_ctx, grad_out, sums_one = first_back(acc, gtwo, hat, inv, ctx, out_weight, order, vecs)
    if near:
        received, grad_ctx = together(swap(up_send, "blk", 1), grad_ctx)
        up = over_cores(up_keep, received)
    grads, give = attend_back(q, k, v, probs, grad_ctx)
    if near:
        up, down, grads, give = together(over_x(up), over_y(down), grads, give)
    back = swap(give, "blk", 1)
    last_keep, last_send = grad_project(
        me, inputs, other_inputs, grads, grad_out, sums_one, sums_two, grad_up_bias, order
    )
    if near:
        up, down, last_keep, last_send = together(
            over_y(up), down[:, 0] + swap(down[:, 1], "dp", 1), last_keep, last_send
        )
        received, gres = together(swap(last_send, "blk", 1), gres)
        last = over_cores(last_keep, received)
    grad_inputs = grad_input_of(gres, grads, back, attn_weights)
    outputs = (output.reshape(tokens.shape), grad_inputs.reshape(tokens.shape))

    if near:
        *got, grad_inputs = together(*z_first(up, down), grad_inputs)
        outputs = (output.reshape(tokens.shape), grad_inputs.reshape(tokens.shape))
        *pair, got_up, got_down = together(*over_first(last), *got)
        one, two, *ends = together(*over_second(pair), *z_second(up, down, got_up, got_down))
        up_sum, down_sum = finish(
            finish_ffn_body, up, down, (got_up, got_down), ends, (), (4 * ROWS, 4 * ROWS), "finish_ffn"
        )
        *got, up_sum = together(*z_first(one, two), up_sum)
        out_sum, query_sum, key_sum, value_sum, vec_sum, bias_sum = finish(
            finish_last_body, one, two, got, z_second(one, two, *got), (order,), (ROWS,) * 4, "finish_last"
        )
        return (
            *outputs,
            query_sum.reshape(-1),
            key_sum.reshape(-1),
            value_sum.reshape(-1),
            out_sum.reshape(-1),
            up_sum.reshape(-1),
            down_sum.reshape(-1),
            bias_sum,
            vec_sum,
        )
    down_sum = scatter(parted(every_group(down_keep, down_send), devices, 4 * own_rows)).astype(f32)
    up_sum = scatter(parted(every_group(up_keep, up_send), devices, own_rows, 4)).astype(f32)
    last = every_group(last_keep, last_send)
    tail = jnp.concatenate(
        (
            last[:, 4 * ROWS, :N_VEC].reshape(devices, n_vec),
            last[:, 4 * ROWS, N_VEC : N_VEC + N_BIAS].reshape(devices, n_bias),
        ),
        axis=1,
    )
    tail = jnp.pad(tail, ((0, 0), (0, D - n_vec - n_bias)))[:, None, :]
    last_sum = scatter(
        jnp.concatenate([parted(last[:, s * ROWS : (s + 1) * ROWS], devices, own_rows) for s in range(4)] + [tail], axis=1)
    ).astype(f32)
    qkv_sum = lax.dot_general(
        last_sum[own_rows : 4 * own_rows],
        order.astype(f32),
        (((1,), (1,)), ((), ())),
        precision=lax.Precision.HIGHEST,
    ).reshape(3, own_rows * D)
    small_sum = last_sum[4 * own_rows]
    return (
        *outputs,
        qkv_sum[0],
        qkv_sum[1],
        qkv_sum[2],
        last_sum[:own_rows].reshape(-1),
        up_sum.reshape(4, own_rows, D).transpose(1, 0, 2).reshape(-1),
        down_sum.reshape(-1),
        small_sum[n_vec : n_vec + n_bias],
        small_sum[:n_vec],
    )


def solution(mesh):
    flat = P(BOTH)
    block = P("dp", "blk", None, None)
    return jax.shard_map(
        body,
        mesh=mesh,
        in_specs=(block, block, P("dp", None), P(), *([flat] * 8)),
        out_specs=(block, block, *([flat] * 8)),
        check_vma=False,
    )
```

```python
from functools import partial

import jax
import jax.numpy as jnp
from jax import lax
from jax.experimental import pallas as pl
from jax.experimental.pallas import tpu as pltpu
from jax.sharding import PartitionSpec as P

D = 768
H = 12
HD = 64
FF = 3072
BLOCK = 512
HALF = D // 2
PAIR = 2 * HD
LANES = 128
GROUPS_W = 32
ROWS = D // GROUPS_W

norm_eps = 1e-05
masked_fill = -1000000000.0
LOG2E = 1.4426950408889634
SQRT_HALF = 0.7071067811865476
INV_SQRT_2PI = 0.3989422804014327

bf16 = jnp.bfloat16
f32 = jnp.float32
BOTH = ("blk", "dp")


def swap(value, axis, mask):
    return lax.ppermute(value, axis, [(source, source ^ mask) for source in range(lax.axis_size(axis))])


def dot_nn(a, b):
    return lax.dot_general(a, b, (((1,), (0,)), ((), ())), preferred_element_type=f32)


def dot_nt(a, b):
    return lax.dot_general(a, b, (((1,), (1,)), ((), ())), preferred_element_type=f32)


def dot_tn(a, b):
    return lax.dot_general(a, b, (((0,), (0,)), ((), ())), preferred_element_type=f32)


def whole(shape):
    return pl.BlockSpec(shape, lambda *_: (0,) * len(shape))


def call(body, grid, in_specs, out_specs, out_shape, scratch=(), prefetch=0, flops=0, moved=0, name=None):
    return pl.pallas_call(
        body,
        grid_spec=pltpu.PrefetchScalarGridSpec(
            num_scalar_prefetch=prefetch,
            grid=grid,
            in_specs=in_specs,
            out_specs=out_specs,
            scratch_shapes=list(scratch),
        ),
        out_shape=out_shape,
        compiler_params=pltpu.CompilerParams(vmem_limit_bytes=60 * 1024 * 1024),
        cost_estimate=pl.CostEstimate(flops=flops, bytes_accessed=moved, transcendentals=0),
        name=name,
    )


def sds(shape, dtype):
    return jax.ShapeDtypeStruct(shape, dtype)


def square(ref):
    return ref[...].reshape(D, D)


PIECES = [(core, y, x) for core in range(2) for y in range(2) for x in range(2)]


def project_body(me_ref, x_ref, xp_ref, *refs):
    pieces, (order_ref, q_ref, k_ref, v_ref, w_ref, out_ref, vec_ref, upb_ref, scr) = refs[: len(PIECES)], refs[len(PIECES) :]

    @pl.when(pl.program_id(0) == 0)
    def _():
        me = me_ref[0]
        total = jnp.zeros((8, D), f32)
        up_bias = jnp.zeros((8, D), f32)
        for (core, y, x), piece in zip(PIECES, pieces):
            for z in range(piece.shape[0]):
                group = (16 * y + 8 * core + 2 * z + x) ^ me
                for part in range(4):
                    scr[part, group] = piece[z, part * ROWS : (part + 1) * ROWS, :]
                total = total + piece[z, 4 * ROWS : 4 * ROWS + 8, :].astype(f32)
                up_bias = up_bias + piece[z, 4 * ROWS + 8 : 4 * ROWS + 16, :].astype(f32)
        vec_ref[...] = total
        upb_ref[...] = up_bias
        for part in range(3):
            w_ref[part] = scr[part].reshape(D, D)
        out_ref[...] = dot_tn(order_ref[...], scr[3].reshape(D, D)).astype(bf16)

    own, other = x_ref[...], xp_ref[...]
    q_ref[...] = (dot_nn(own, w_ref[0]) + vec_ref[0:1, :]).astype(bf16)
    k_ref[:, :HALF] = dot_nn(other, w_ref[1, :, :HALF]).astype(bf16)
    k_ref[:, HALF:] = dot_nn(own, w_ref[1, :, HALF:]).astype(bf16)
    v_ref[:, :HALF] = (dot_nn(other, w_ref[2, :, :HALF]) + vec_ref[1:2, :HALF]).astype(bf16)
    v_ref[:, HALF:] = (dot_nn(own, w_ref[2, :, HALF:]) + vec_ref[1:2, HALF:]).astype(bf16)


def project(me, x, xp, pieces, order):
    rows = x.shape[0]
    step = BLOCK
    row_spec = pl.BlockSpec((step, D), lambda i, *_: (i, 0))
    return call(
        project_body,
        (rows // step,),
        [row_spec, row_spec] + [whole(pieces[0].shape)] * len(PIECES) + [whole((D, D))],
        [row_spec] * 3 + [whole((3, D, D)), whole((D, D)), whole((8, D)), whole((8, D))],
        [sds((rows, D), bf16)] * 3 + [sds((3, D, D), bf16), sds((D, D), bf16), sds((8, D), f32), sds((8, D), f32)],
        scratch=[pltpu.VMEM((4, GROUPS_W, ROWS, D), bf16)],
        prefetch=1,
        flops=6 * rows * D * D,
        moved=10 * rows * D + 12 * D * D,
        name="project",
    )(me, x, xp, *pieces, order)


def attend_body(valid_ref, q_ref, k_ref, v_ref, ctx_ref, p_ref):
    seq, pair = pl.program_id(0), pl.program_id(1)
    valid = valid_ref[seq, pair // 3]
    queries, keys, values = q_ref[...], k_ref[...], v_ref[...]
    lane = lax.broadcasted_iota(jnp.int32, (BLOCK, PAIR), 1)
    key_row = lax.broadcasted_iota(jnp.int32, (BLOCK, 1), 0)
    fill = jnp.where(key_row < valid, 0.0, masked_fill * LOG2E)
    parts = []
    for head in range(2):
        mine = (lane < HD) if head == 0 else (lane >= HD)
        masked = jnp.where(mine, queries, jnp.zeros_like(queries))
        scores = dot_nt(keys, masked) * (LOG2E * HD ** (-0.5)) + fill
        top = jnp.max(scores, axis=0, keepdims=True)
        weights = jnp.exp2(scores - top)
        total = jnp.sum(weights, axis=0, keepdims=True)
        probs = (weights * (1.0 / total)).astype(bf16)
        p_ref[0, head] = probs
        parts.append(dot_tn(probs, values))
    ctx_ref[...] = jnp.where(lane < HD, parts[0], parts[1]).astype(bf16)


def attend(valid, q, k, v):
    rows = q.shape[0]
    seqs = rows // BLOCK
    spec = pl.BlockSpec((BLOCK, PAIR), lambda s, j, *_: (s, j))
    return call(
        attend_body,
        (seqs, H // 2),
        [spec] * 3,
        [spec, pl.BlockSpec((1, 2, BLOCK, BLOCK), lambda s, j, *_: (s, j, 0, 0))],
        [sds((rows, D), bf16), sds((seqs, H, BLOCK, BLOCK), bf16)],
        prefetch=1,
        flops=16 * rows * BLOCK * D,
        moved=8 * rows * D + 2 * rows * H * BLOCK,
        name="attend",
    )(valid, q, k, v)


def attend_back_body(q_ref, k_ref, v_ref, p_ref, gctx_ref, out_ref, give_ref):
    pair = pl.program_id(1)
    queries, keys, values, grad_ctx = q_ref[...], k_ref[...], v_ref[...], gctx_ref[...]
    lane = lax.broadcasted_iota(jnp.int32, (BLOCK, PAIR), 1)
    scale = HD ** (-0.5)
    gq, gk, gv = [], [], []
    for head in range(2):
        mine = (lane < HD) if head == 0 else (lane >= HD)
        probs = p_ref[0, head]
        grad_probs = dot_nt(jnp.where(mine, values, jnp.zeros_like(values)), grad_ctx)
        delta = jnp.sum(probs.astype(f32) * grad_probs, axis=0, keepdims=True)
        grad_scores = (probs.astype(f32) * (grad_probs - delta)).astype(bf16)
        gv.append(dot_nn(probs, grad_ctx))
        gk.append(dot_nn(grad_scores, queries))
        gq.append(dot_tn(grad_scores, keys))
    first = lane < HD
    out_ref[0] = (jnp.where(first, gq[0], gq[1]) * scale).astype(bf16)
    grad_keys = (jnp.where(first, gk[0], gk[1]) * scale).astype(bf16)
    grad_values = jnp.where(first, gv[0], gv[1]).astype(bf16)
    out_ref[1] = grad_keys
    out_ref[2] = grad_values

    @pl.when(pair < H // 4)
    def _():
        give_ref[0] = grad_keys
        give_ref[1] = grad_values


def attend_back(q, k, v, probs, grad_ctx):
    rows = q.shape[0]
    seqs = rows // BLOCK
    spec = pl.BlockSpec((BLOCK, PAIR), lambda s, j: (s, j))
    return call(
        attend_back_body,
        (seqs, H // 2),
        [spec] * 3
        + [
            pl.BlockSpec((1, 2, BLOCK, BLOCK), lambda s, j: (s, j, 0, 0)),
            spec,
        ],
        [
            pl.BlockSpec((3, BLOCK, PAIR), lambda s, j: (0, s, j)),
            pl.BlockSpec((2, BLOCK, PAIR), lambda s, j: (0, s, jnp.minimum(j, H // 4 - 1))),
        ],
        [sds((3, rows, D), bf16), sds((2, rows, HALF), bf16)],
        flops=32 * rows * BLOCK * D,
        moved=14 * rows * D + 2 * rows * H * BLOCK,
        name="attend_back",
    )(q, k, v, probs, grad_ctx)


def mean_last(value):
    return jnp.sum(value, axis=-1, keepdims=True) * (1.0 / D)


def first_norm_body(ctx_ref, x_ref, wop_ref, vec_ref, hat_ref, inv_ref, low_ref):
    branch = dot_nn(ctx_ref[...], wop_ref[...]) + vec_ref[2:3, :]
    residual = x_ref[...].astype(f32) + branch
    centred = residual - mean_last(residual)
    inv = lax.rsqrt(mean_last(centred * centred) + norm_eps)
    hat = centred * inv
    hat_ref[...] = hat
    inv_ref[...] = jnp.broadcast_to(inv, inv_ref.shape)
    low_ref[...] = (hat * vec_ref[3:4, :] + vec_ref[4:5, :]).astype(bf16)


def first_norm(ctx, x, wop, vecs):
    rows = x.shape[0]
    step = BLOCK
    row_spec = pl.BlockSpec((step, D), lambda i: (i, 0))
    return call(
        first_norm_body,
        (rows // step,),
        [row_spec, row_spec, whole((D, D)), whole((8, D))],
        [row_spec, pl.BlockSpec((step, LANES), lambda i: (i, 0)), row_spec],
        [sds((rows, D), f32), sds((rows, LANES), f32), sds((rows, D), bf16)],
        flops=2 * rows * D * D,
        moved=12 * rows * D,
        name="first_norm",
    )(ctx, x, wop, vecs)


def gelu_and_slope(value):
    size = jnp.abs(value)
    gauss = jnp.exp2(value * value * (-0.5 * LOG2E))
    knot = 1.0 / (1.0 + size * (0.3275911 * SQRT_HALF))
    poly = knot * (
        0.254829592 + knot * (-0.284496736 + knot * (1.421413741 + knot * (-1.453152027 + knot * 1.061405429)))
    )
    tail = 0.5 * poly * gauss
    normal_cdf = jnp.where(value >= 0.0, 1.0 - tail, tail)
    return value * normal_cdf, normal_cdf + value * gauss * INV_SQRT_2PI


def ffn_forward_body(
    low_ref, hat_ref, cot_ref, up_ref, down_ref, bias_ref, vec_ref,
    act_ref, slope_ref, out_ref, gtwo_ref, gsec_ref, sums_ref, acc,
):
    chunk, last = pl.program_id(1), pl.num_programs(1) - 1
    first = (pl.program_id(0) == 0) & (chunk == 0)
    rows = low_ref.shape[0]
    step = 256
    w_up = square(up_ref)
    w_down = square(down_ref)

    @pl.when(first)
    def _():
        sums_ref[...] = jnp.zeros_like(sums_ref)

    @pl.when(chunk == 0)
    def _():
        acc[...] = jnp.zeros_like(acc)

    for start in range(0, rows, step):
        part = pl.ds(start, step)
        hidden = dot_nn(low_ref[part, :], w_up) + bias_ref[pl.ds(chunk, 1), :]
        activated, slope = gelu_and_slope(hidden)
        activated = activated.astype(bf16)
        act_ref[part, :] = activated
        slope_ref[part, :] = slope.astype(bf16)
        down = dot_nn(activated, w_down)

        acc[part, :] += down

    @pl.when(chunk == last)
    def _():
        gain, bias = vec_ref[6:7, :], vec_ref[7:8, :]

        def rows_of(index, sums):
            part = pl.ds(pl.multiple_of(index * step, step), step)
            residual = hat_ref[part, :] * vec_ref[3:4, :] + vec_ref[4:5, :] + (acc[part, :] + vec_ref[5:6, :])
            centred = residual - mean_last(residual)
            inv = lax.rsqrt(mean_last(centred * centred) + norm_eps)
            hat = centred * inv
            out_ref[part, :] = (hat * gain + bias).astype(bf16)
            cot = cot_ref[part, :].astype(f32)
            scaled = cot * gain
            grad = inv * (scaled - mean_last(scaled) - hat * mean_last(scaled * hat))
            gtwo_ref[part, :] = grad
            low = grad.astype(bf16)
            gsec_ref[part, :] = low
            return (
                sums[0] + jnp.sum(cot * hat, axis=0, keepdims=True),
                sums[1] + jnp.sum(cot, axis=0, keepdims=True),
                sums[2] + jnp.sum(low.astype(f32), axis=0, keepdims=True),
            )

        zero = jnp.zeros((1, D), f32)
        sums = lax.fori_loop(0, rows // step, rows_of, (zero, zero, zero))
        for index, value in enumerate(sums):
            sums_ref[index : index + 1, :] += value


def ffn_forward(low, hat, cot, pack, up_bias, vecs):
    rows = low.shape[0]
    span = 1024
    chunks = FF // D
    row_spec = pl.BlockSpec((span, D), lambda r, c: (r, 0))
    wide = pl.BlockSpec((span, D), lambda r, c: (r, c))
    return call(
        ffn_forward_body,
        (rows // span, chunks),
        [
            row_spec,
            row_spec,
            row_spec,
            pl.BlockSpec((GROUPS_W, ROWS, D), lambda r, c: (0, 4 + c, 0)),
            pl.BlockSpec((GROUPS_W // 4, 4 * ROWS, D), lambda r, c: (c, 0, 0)),
            whole((8, D)),
            whole((8, D)),
        ],
        [wide, wide, row_spec, row_spec, row_spec, whole((8, D))],
        [
            sds((rows, FF), bf16),
            sds((rows, FF), bf16),
            sds((rows, D), bf16),
            sds((rows, D), f32),
            sds((rows, D), bf16),
            sds((8, D), f32),
        ],
        scratch=[pltpu.VMEM((span, D), f32)],
        flops=4 * rows * D * FF,
        moved=26 * rows * D + 4 * D * FF,
        name="ffn_forward",
    )(low, hat, cot, pack, pack, up_bias, vecs)


def grad_down_body(me_ref, act_ref, gsec_ref, keep_ref, send_ref, scr):
    step = pl.program_id(0)
    scr[...] = dot_tn(act_ref[...], gsec_ref[...]).astype(bf16).reshape(scr.shape)
    place = jnp.bitwise_and(me_ref[0], 7)

    @pl.when(step < 2)
    def _():
        for index in range(8):
            keep_ref[0, index] = scr[place ^ index]

    @pl.when(step >= 2)
    def _():
        for index in range(8):
            send_ref[0, index] = scr[place ^ index]


def grad_down_of(me, act, gsec):
    rows = act.shape[0]
    block = (1, GROUPS_W // 4, 4 * ROWS, D)
    return call(
        grad_down_body,
        (FF // D,),
        [
            pl.BlockSpec((rows, D), lambda s, me_ref: (0, ((s % 2) * 2 + s // 2) ^ (me_ref[0] // 8))),
            whole((rows, D)),
        ],
        [
            pl.BlockSpec(block, lambda s, me_ref: (jnp.minimum(s, 1), 0, 0, 0)),
            pl.BlockSpec(block, lambda s, me_ref: (jnp.maximum(s - 2, 0), 0, 0, 0)),
        ],
        [sds((2, *block[1:]), bf16)] * 2,
        scratch=[pltpu.VMEM(block[1:], bf16)],
        prefetch=1,
        flops=2 * rows * D * FF,
        moved=10 * rows * D + 2 * D * FF,
        name="grad_down",
    )(me, act, gsec)


def apart(scr, me, keep, send):
    def one(index, carry):
        group = (2 * index - jnp.bitwise_and(index, 7)) ^ me
        keep(index, scr[group])
        send(index, scr[group ^ 8])
        return carry

    lax.fori_loop(0, GROUPS_W // 2, one, 0)


def ffn_backward_body(
    me_ref, gsec_ref, slope_ref, low_ref, up_ref, down_ref, keep_ref, send_ref, gbias_ref, acc_ref, scr
):
    chunk = pl.program_id(0)
    grad_act = dot_nt(gsec_ref[...], square(down_ref))
    grad_hidden = (grad_act * slope_ref[...].astype(f32)).astype(bf16)
    gbias_ref[0] = jnp.sum(grad_hidden.astype(f32), axis=0, keepdims=True)
    scr[...] = dot_tn(low_ref[...], grad_hidden).astype(bf16).reshape(scr.shape)

    def keep(index, value):
        keep_ref[index] = value

    def send(index, value):
        send_ref[index] = value

    apart(scr, me_ref[0], keep, send)
    back = dot_nt(grad_hidden, square(up_ref))

    @pl.when(chunk == 0)
    def _():
        acc_ref[...] = back

    @pl.when(chunk > 0)
    def _():
        acc_ref[...] += back


def ffn_backward(me, gsec, slope, low, pack):
    rows = gsec.shape[0]
    half = pl.BlockSpec((GROUPS_W // 2, ROWS, D), lambda c, *_: (0, c, 0))
    return call(
        ffn_backward_body,
        (FF // D,),
        [
            whole((rows, D)),
            pl.BlockSpec((rows, D), lambda c, *_: (0, c)),
            whole((rows, D)),
            pl.BlockSpec((GROUPS_W, ROWS, D), lambda c, *_: (0, 4 + c, 0)),
            pl.BlockSpec((GROUPS_W // 4, 4 * ROWS, D), lambda c, *_: (c, 0, 0)),
        ],
        [half, half, pl.BlockSpec((1, 1, D), lambda c, *_: (c, 0, 0)), whole((rows, D))],
        [sds((GROUPS_W // 2, 4 * ROWS, D), bf16)] * 2 + [sds((FF // D, 1, D), f32), sds((rows, D), f32)],
        scratch=[pltpu.VMEM((GROUPS_W, ROWS, D), bf16)],
        prefetch=1,
        flops=6 * rows * D * FF,
        moved=16 * rows * D + 6 * D * FF,
        name="ffn_backward",
    )(me, gsec, slope, low, pack, pack)


def first_back_body(
    acc_ref, gtwo_ref, hat_ref, inv_ref, ctx_ref, wop_ref, order_ref, vec_ref,
    gres_ref, gctx_ref, gout_ref, sums_ref, gout_scr,
):
    index, last = pl.program_id(0), pl.num_programs(0) - 1
    hat = hat_ref[...]
    inv = inv_ref[:, 0:1]
    grad_first = gtwo_ref[...] + acc_ref[...]
    scaled = grad_first * vec_ref[3:4, :]
    grad = inv * (scaled - mean_last(scaled) - hat * mean_last(scaled * hat))
    gres_ref[...] = grad
    low = grad.astype(bf16)
    ctx = ctx_ref[...]
    gctx_ref[...] = dot_nt(low, wop_ref[...]).astype(bf16)
    grad_out = dot_tn(ctx, low)

    @pl.when(index == 0)
    def _():
        gout_scr[...] = grad_out
        sums_ref[...] = jnp.zeros_like(sums_ref)

    @pl.when(index > 0)
    def _():
        gout_scr[...] += grad_out

    sums_ref[0:1, :] += jnp.sum(grad_first * hat, axis=0, keepdims=True)
    sums_ref[1:2, :] += jnp.sum(grad_first, axis=0, keepdims=True)
    sums_ref[2:3, :] += jnp.sum(low.astype(f32), axis=0, keepdims=True)

    @pl.when(index == last)
    def _():
        ordered = dot_nn(order_ref[...], gout_scr[...].astype(bf16))
        gout_ref[...] = ordered.astype(bf16).reshape(gout_ref.shape)


def first_back(acc, gtwo, hat, inv, ctx, wop, order, vecs):
    rows = acc.shape[0]
    step = 2 * BLOCK
    row_spec = pl.BlockSpec((step, D), lambda i: (i, 0))
    return call(
        first_back_body,
        (rows // step,),
        [
            row_spec,
            row_spec,
            row_spec,
            pl.BlockSpec((step, LANES), lambda i: (i, 0)),
            row_spec,
            whole((D, D)),
            whole((D, D)),
            whole((8, D)),
        ],
        [
            row_spec,
            row_spec,
            whole((GROUPS_W, ROWS, D)),
            whole((8, D)),
        ],
        [
            sds((rows, D), f32),
            sds((rows, D), bf16),
            sds((GROUPS_W, ROWS, D), bf16),
            sds((8, D), f32),
        ],
        scratch=[pltpu.VMEM((D, D), f32)],
        flops=4 * rows * D * D,
        moved=20 * rows * D + 6 * D * D,
        name="first_back",
    )(acc, gtwo, hat, inv, ctx, wop, order, vecs)


def in_order(rows, order):
    high = rows.astype(bf16)
    rest = rows - high.astype(f32)
    middle = rest.astype(bf16)
    low = (rest - middle.astype(f32)).astype(bf16)
    return dot_nt(high, order) + (dot_nt(middle, order) + dot_nt(low, order))


LAST_ROWS = 4 * ROWS + 8
N_VEC = 8 * D // GROUPS_W
N_BIAS = FF // GROUPS_W


def grad_project_body(
    me_ref, x_ref, xp_ref, grad_ref, gout_ref, one_ref, two_ref, upb_ref, order_ref, keep_ref, send_ref, scr, sums, small
):
    part = pl.program_id(0)
    me = me_ref[0]
    own = x_ref[...]
    other = jnp.where(part == 0, own, xp_ref[...])
    grad = grad_ref[0]
    left = dot_tn(other, grad[:, :HALF]).astype(bf16)
    right = dot_tn(own, grad[:, HALF:]).astype(bf16)
    scr[:, :, :HALF] = left.reshape(GROUPS_W, ROWS, HALF)
    scr[:, :, HALF:] = right.reshape(GROUPS_W, ROWS, HALF)
    sums[pl.ds(part, 1), :] = jnp.sum(grad.astype(f32), axis=0, keepdims=True)

    def place(source, start, size):
        def keep(index, value):
            keep_ref[index, start : start + size, :] = value.astype(bf16)

        def send(index, value):
            send_ref[index, start : start + size, :] = value.astype(bf16)

        apart(source, me, keep, send)

    for index in range(3):

        @pl.when(part == index)
        def _():
            place(scr, (index + 1) * ROWS, ROWS)

    @pl.when(part == 0)
    def _():
        place(gout_ref, 0, ROWS)

    @pl.when(part == 2)
    def _():
        bias = in_order(sums[...], order_ref[...])
        rows = (
            bias[0:1], bias[2:3], one_ref[2:3, :], one_ref[0:1, :],
            one_ref[1:2, :], two_ref[2:3, :], two_ref[0:1, :], two_ref[1:2, :],
        )
        small[...] = jnp.zeros_like(small)
        for group in range(GROUPS_W):
            row, column = divmod(group, GROUPS_W // 8)
            small[group, 0:1, :N_VEC] = rows[row][:, column * N_VEC : (column + 1) * N_VEC]
            row, column = divmod(group, GROUPS_W // 4)
            small[group, 0:1, N_VEC : N_VEC + N_BIAS] = upb_ref[row, :, column * N_BIAS : (column + 1) * N_BIAS]
        place(small, 4 * ROWS, 8)


def grad_project(me, x, xp, grads, grad_out, sums_one, sums_two, up_bias, order):
    rows = x.shape[0]
    half = (GROUPS_W // 2, LAST_ROWS, D)
    return call(
        grad_project_body,
        (3,),
        [
            whole((rows, D)),
            whole((rows, D)),
            pl.BlockSpec((1, rows, D), lambda s, *_: (s, 0, 0)),
            whole((GROUPS_W, ROWS, D)),
            whole((8, D)),
            whole((8, D)),
            whole((FF // D, 1, D)),
            whole((D, D)),
        ],
        [whole(half)] * 2,
        [sds(half, bf16)] * 2,
        scratch=[
            pltpu.VMEM((GROUPS_W, ROWS, D), bf16),
            pltpu.VMEM((8, D), f32),
            pltpu.VMEM((GROUPS_W, 8, D), f32),
        ],
        prefetch=1,
        flops=6 * rows * D * D,
        moved=10 * rows * D + 12 * D * D,
        name="grad_project",
    )(me, x, xp, grads, grad_out, sums_one, sums_two, up_bias, order)


def grad_input_body(gres_ref, grads_ref, back_ref, w_ref, out_ref):
    total = gres_ref[...] + dot_nt(grads_ref[0], w_ref[0])
    for part in (1, 2):
        total = total + dot_nt(back_ref[part - 1], w_ref[part, :, :HALF])
        total = total + dot_nt(grads_ref[part, :, HALF:], w_ref[part, :, HALF:])
    out_ref[...] = total


def grad_input_of(gres, grads, back, weights):
    rows = gres.shape[0]
    step = 256
    row_spec = pl.BlockSpec((step, D), lambda i: (i, 0))
    return call(
        grad_input_body,
        (rows // step,),
        [
            row_spec,
            pl.BlockSpec((3, step, D), lambda i: (0, i, 0)),
            pl.BlockSpec((2, step, HALF), lambda i: (0, i, 0)),
            whole((3, D, D)),
        ],
        row_spec,
        sds((rows, D), f32),
        flops=6 * rows * D * D,
        moved=16 * rows * D + 6 * D * D,
        name="grad_input",
    )(gres, grads, back, weights)


def summed(refs, start, stop):
    total = refs[0][start:stop, :].astype(f32)
    for ref in refs[1:]:
        total = total + ref[start:stop, :].astype(f32)
    return total


def spread(out_ref, total, first, stride):
    for column in range(D // LANES):
        out_ref[pl.ds(first + column, total.shape[0], stride=stride), :] = total[:, column * LANES : (column + 1) * LANES]


def finish_ffn_body(*refs):
    up_ref, down_ref = refs[6:]
    for chunk in range(4):
        spread(up_ref, summed(refs[:3], chunk * ROWS, (chunk + 1) * ROWS), chunk * (D // LANES), FF // LANES)
    spread(down_ref, summed(refs[3:6], 0, 4 * ROWS), 0, D // LANES)


def finish_last_body(*refs):
    order_ref, out_ref, q_ref, k_ref, v_ref, vec_ref, upb_ref = refs[6:]
    one, two = refs[:3], refs[3:6]
    half = one[0].shape[0]
    spread(out_ref, summed(one, 0, ROWS), 0, D // LANES)
    middle = jnp.concatenate((summed(one, ROWS, half), summed(two, 0, 4 * ROWS - half)), axis=0)
    ordered = in_order(middle, order_ref[...])
    for part, ref in enumerate((q_ref, k_ref, v_ref)):
        spread(ref, ordered[part * ROWS : (part + 1) * ROWS], 0, D // LANES)
    small = summed(two, 4 * ROWS - half, 4 * ROWS - half + 8)
    vec_ref[...] = small[0, :N_VEC]
    upb_ref[...] = small[0, N_VEC : N_VEC + N_BIAS]


def z_first(one, two):
    return swap(one[1:3], "dp", 2), swap(two[2:4], "dp", 6)


def z_second(one, two, got_one, got_two):
    return swap(one[3] + got_one[1], "dp", 6), swap(two[1] + got_two[0], "dp", 2)


def finish(body, one, two, got, last, extra, sizes, name):
    shapes = [(size * D // LANES, LANES) for size in sizes]
    if extra:
        shapes = shapes + [(N_VEC,), (N_BIAS,)]

    def piece(value, index):
        return pl.BlockSpec((None, *value.shape[1:]), lambda i: (index, 0, 0))

    return call(
        body,
        (1,),
        [piece(one, 0), piece(got[0], 0), whole(last[0].shape), piece(two, 0), piece(got[1], 1), whole(last[1].shape)]
        + [whole(value.shape) for value in extra],
        [whole(shape) for shape in shapes],
        [sds(shape, f32) for shape in shapes],
        moved=8 * (one.shape[1] + two.shape[1]) * D,
        name=name,
    )(one, got[0], last[0], two, got[1], last[1], *extra)


def gather(value):
    return lax.all_gather(value, BOTH, axis=0)


def scatter(value):
    return lax.psum_scatter(value, BOTH, scatter_dimension=0)


def joined(gathered, start, rows, columns=1):
    count = gathered.shape[0]
    part = gathered[:, start : start + columns * rows]
    if columns > 1:
        part = part.reshape(GROUPS_W, count // GROUPS_W, columns, rows, D).transpose(0, 2, 1, 3, 4)
    return part.reshape(GROUPS_W, -1, D)


def parted(grouped, count, rows, columns=1):
    if columns > 1:
        grouped = grouped.reshape(GROUPS_W, columns, count // GROUPS_W, rows, D).transpose(0, 2, 1, 3, 4)
    return grouped.reshape(count, columns * rows, D)


def gather_near(shard):
    rows = shard.shape[0]
    half = rows // 16 * 8
    one, three = swap(shard, "dp", 2), swap(shard, "dp", 6)
    two = jnp.concatenate((swap(three[:half], "dp", 2), swap(one[half:], "dp", 6)))
    column = jnp.stack((shard, one, two, three))
    over_x = swap(column, "dp", 1)
    over_y = swap(column, "blk", 2)
    over_both = jnp.concatenate((swap(over_y[:, :half], "dp", 1), swap(over_x[:, half:], "blk", 2)), axis=1)
    near = {(0, 0): column, (0, 1): over_x, (1, 0): over_y, (1, 1): over_both}
    pieces = {(0, y, x): value for (y, x), value in near.items()}
    pieces.update({(1, y, x): swap(value, "blk", 1) for (y, x), value in near.items()})
    return [pieces[key] for key in PIECES]


def over_cores(keep, received):
    return (keep + received).reshape(2, 4, 2, keep.shape[1], D)


def over_x(total):
    return total[:, :, 0] + swap(total[:, :, 1], "dp", 1)


def over_y(total):
    return total[0] + swap(total[1], "blk", 2)


def over_first(total):
    rows = total.shape[3]
    half = (rows + 8) // 16 * 8
    one, two = total[:, :, :, :half], total[:, :, :, half:]
    return one[:, :, 0] + swap(one[:, :, 1], "dp", 1), two[0] + swap(two[1], "blk", 2)


def over_second(pair):
    one, two = pair
    one = one[0] + swap(one[1], "blk", 2)
    two = two[:, 0] + swap(two[:, 1], "dp", 1)
    return one, two


def together(*values):
    return lax.optimization_barrier(values)


def every_group(keep, send):
    rows = keep.shape[1]
    return jnp.stack((keep.reshape(2, 8, rows, D), send.reshape(2, 8, rows, D)), axis=1).reshape(GROUPS_W, rows, D)


def body(tokens, cotangent, lengths, head_mode, w_query, w_key, w_value, w_out, w_up, w_down, b_up, vectors):
    seq_count = tokens.shape[0]
    row_count = seq_count * BLOCK
    devices = lax.axis_size("blk") * lax.axis_size("dp")
    near = devices == GROUPS_W
    own_rows = D // devices
    n_vec, n_bias = vectors.shape[0], b_up.shape[0]
    blk_index = lax.axis_index("blk")
    device = blk_index * lax.axis_size("dp") + lax.axis_index("dp")
    me = (device if near else device * 0).reshape(1).astype(jnp.int32)
    block_side = blk_index % 2
    member = blk_index // 2
    seq_lengths = jnp.where(member == 0, lengths[:, 0], lengths[:, 1])
    valid = jnp.stack(
        (
            jnp.clip(seq_lengths - (1 - block_side) * BLOCK, 0, BLOCK),
            jnp.clip(seq_lengths - block_side * BLOCK, 0, BLOCK),
        ),
        axis=1,
    ).astype(jnp.int32)
    swapped = head_mode == 1
    place = jnp.where(swapped, jnp.cumsum(swapped) - 1, H // 2 + jnp.cumsum(~swapped) - 1)
    target = jnp.repeat(place * HD, HD) + jnp.tile(jnp.arange(HD), H)
    order = (target[:, None] == jnp.arange(D)[None, :]).astype(bf16)

    inputs = tokens.reshape(row_count, D)
    other_inputs = swap(inputs, "blk", 1)

    ffn_shard = jnp.concatenate(
        (
            w_down.reshape(4 * own_rows, D),
            w_up.reshape(own_rows, 4, D).transpose(1, 0, 2).reshape(4 * own_rows, D),
        )
    )
    ffn_pack = gather(ffn_shard)
    up_bias = lax.dynamic_update_slice(jnp.zeros((8 * D,), bf16), b_up, (device * n_bias,)).reshape(8, D)
    small = lax.dynamic_update_slice(jnp.zeros((8 * D,), bf16), vectors, (device * n_vec,)).reshape(8, D)
    stacked = jnp.concatenate([w.reshape(own_rows, D) for w in (w_query, w_key, w_value)] + [small[0:2]])
    stacked = dot_nn(stacked, order).astype(bf16)
    attn_shard = jnp.concatenate(
        (stacked[: 3 * own_rows], w_out.reshape(own_rows, D), stacked[3 * own_rows :], small[2:], up_bias)
    )
    if near:
        pieces = gather_near(attn_shard)
    else:
        attn_all = gather(attn_shard)
        attn_pack = jnp.concatenate(
            [joined(attn_all, s * own_rows, own_rows) for s in range(4)]
            + [jnp.sum(attn_all[:, 4 * own_rows :].reshape(GROUPS_W, -1, 16, D), axis=1)],
            axis=1,
        ).reshape(2, 2, 4, 2, 4 * ROWS + 16, D)
        pieces = [attn_pack[y, core, :, x] for core, y, x in PIECES]
        ffn_pack = jnp.concatenate(
            (joined(ffn_pack, 0, 4 * own_rows), joined(ffn_pack, 4 * own_rows, own_rows, 4)), axis=1
        )

    q, k, v, attn_weights, out_weight, vecs, up_biases = project(me, inputs, other_inputs, pieces, order)
    ctx, probs = attend(valid, q, k, v)
    hat, inv, low = first_norm(ctx, inputs, out_weight, vecs)
    act, slope, output, gtwo, gsec, sums_two = ffn_forward(
        low, hat, cotangent.reshape(row_count, D), ffn_pack, up_biases, vecs
    )
    down_keep, down_send = grad_down_of(me, act, gsec)
    down_keep, down_send = (value.reshape(GROUPS_W // 2, 4 * ROWS, D) for value in (down_keep, down_send))
    down_keep, down_send, gsec = together(down_keep, down_send, gsec)
    up_keep, up_send, grad_up_bias, acc = ffn_backward(me, gsec, slope, low, ffn_pack)
    if near:
        received, acc = together(swap(down_send, "blk", 1), acc)
        down = over_cores(down_keep, received)
    gres, grad_ctx, grad_out, sums_one = first_back(acc, gtwo, hat, inv, ctx, out_weight, order, vecs)
    if near:
        received, grad_ctx = together(swap(up_send, "blk", 1), grad_ctx)
        up = over_cores(up_keep, received)
    grads, give = attend_back(q, k, v, probs, grad_ctx)
    if near:
        up, down, grads, give = together(over_x(up), over_y(down), grads, give)
    back = swap(give, "blk", 1)
    last_keep, last_send = grad_project(
        me, inputs, other_inputs, grads, grad_out, sums_one, sums_two, grad_up_bias, order
    )
    if near:
        up, down, last_keep, last_send = together(
            over_y(up), down[:, 0] + swap(down[:, 1], "dp", 1), last_keep, last_send
        )
        received, gres = together(swap(last_send, "blk", 1), gres)
        last = over_cores(last_keep, received)
    grad_inputs = grad_input_of(gres, grads, back, attn_weights)
    outputs = (output.reshape(tokens.shape), grad_inputs.reshape(tokens.shape))

    if near:
        *got, grad_inputs = together(*z_first(up, down), grad_inputs)
        outputs = (output.reshape(tokens.shape), grad_inputs.reshape(tokens.shape))
        *pair, got_up, got_down = together(*over_first(last), *got)
        one, two, *ends = together(*over_second(pair), *z_second(up, down, got_up, got_down))
        up_sum, down_sum = finish(
            finish_ffn_body, up, down, (got_up, got_down), ends, (), (4 * ROWS, 4 * ROWS), "finish_ffn"
        )
        *got, up_sum = together(*z_first(one, two), up_sum)
        out_sum, query_sum, key_sum, value_sum, vec_sum, bias_sum = finish(
            finish_last_body, one, two, got, z_second(one, two, *got), (order,), (ROWS,) * 4, "finish_last"
        )
        return (
            *outputs,
            query_sum.reshape(-1),
            key_sum.reshape(-1),
            value_sum.reshape(-1),
            out_sum.reshape(-1),
            up_sum.reshape(-1),
            down_sum.reshape(-1),
            bias_sum,
            vec_sum,
        )
    down_sum = scatter(parted(every_group(down_keep, down_send), devices, 4 * own_rows)).astype(f32)
    up_sum = scatter(parted(every_group(up_keep, up_send), devices, own_rows, 4)).astype(f32)
    last = every_group(last_keep, last_send)
    tail = jnp.concatenate(
        (
            last[:, 4 * ROWS, :N_VEC].reshape(devices, n_vec),
            last[:, 4 * ROWS, N_VEC : N_VEC + N_BIAS].reshape(devices, n_bias),
        ),
        axis=1,
    )
    tail = jnp.pad(tail, ((0, 0), (0, D - n_vec - n_bias)))[:, None, :]
    last_sum = scatter(
        jnp.concatenate([parted(last[:, s * ROWS : (s + 1) * ROWS], devices, own_rows) for s in range(4)] + [tail], axis=1)
    ).astype(f32)
    qkv_sum = lax.dot_general(
        last_sum[own_rows : 4 * own_rows],
        order.astype(f32),
        (((1,), (1,)), ((), ())),
        precision=lax.Precision.HIGHEST,
    ).reshape(3, own_rows * D)
    small_sum = last_sum[4 * own_rows]
    return (
        *outputs,
        qkv_sum[0],
        qkv_sum[1],
        qkv_sum[2],
        last_sum[:own_rows].reshape(-1),
        up_sum.reshape(4, own_rows, D).transpose(1, 0, 2).reshape(-1),
        down_sum.reshape(-1),
        small_sum[n_vec : n_vec + n_bias],
        small_sum[:n_vec],
    )


def solution(mesh):
    flat = P(BOTH)
    block = P("dp", "blk", None, None)
    return jax.shard_map(
        body,
        mesh=mesh,
        in_specs=(block, block, P("dp", None), P(), *([flat] * 8)),
        out_specs=(block, block, *([flat] * 8)),
        check_vma=False,
    )
```

```python
from functools import partial

import jax
import jax.numpy as jnp
from jax import lax
from jax.experimental import pallas as pl
from jax.experimental.pallas import tpu as pltpu
from jax.sharding import PartitionSpec as P

D = 768
H = 12
HD = 64
FF = 3072
BLOCK = 512
HALF = D // 2
PAIR = 2 * HD
LANES = 128
GROUPS_W = 32
ROWS = D // GROUPS_W

norm_eps = 1e-05
masked_fill = -1000000000.0
LOG2E = 1.4426950408889634
SQRT_HALF = 0.7071067811865476
INV_SQRT_2PI = 0.3989422804014327

bf16 = jnp.bfloat16
f32 = jnp.float32
BOTH = ("blk", "dp")


def swap(value, axis, mask):
    return lax.ppermute(value, axis, [(source, source ^ mask) for source in range(lax.axis_size(axis))])


def dot_nn(a, b):
    return lax.dot_general(a, b, (((1,), (0,)), ((), ())), preferred_element_type=f32)


def dot_nt(a, b):
    return lax.dot_general(a, b, (((1,), (1,)), ((), ())), preferred_element_type=f32)


def dot_tn(a, b):
    return lax.dot_general(a, b, (((0,), (0,)), ((), ())), preferred_element_type=f32)


def whole(shape):
    return pl.BlockSpec(shape, lambda *_: (0,) * len(shape))


def call(body, grid, in_specs, out_specs, out_shape, scratch=(), prefetch=0, flops=0, moved=0, name=None):
    return pl.pallas_call(
        body,
        grid_spec=pltpu.PrefetchScalarGridSpec(
            num_scalar_prefetch=prefetch,
            grid=grid,
            in_specs=in_specs,
            out_specs=out_specs,
            scratch_shapes=list(scratch),
        ),
        out_shape=out_shape,
        compiler_params=pltpu.CompilerParams(vmem_limit_bytes=60 * 1024 * 1024),
        cost_estimate=pl.CostEstimate(flops=flops, bytes_accessed=moved, transcendentals=0),
        name=name,
    )


def sds(shape, dtype):
    return jax.ShapeDtypeStruct(shape, dtype)


def square(ref):
    return ref[...].reshape(D, D)


PIECES = [(core, y, x) for core in range(2) for y in range(2) for x in range(2)]


def project_body(me_ref, x_ref, xp_ref, *refs):
    pieces, (order_ref, q_ref, k_ref, v_ref, w_ref, out_ref, vec_ref, upb_ref, scr) = refs[: len(PIECES)], refs[len(PIECES) :]

    @pl.when(pl.program_id(0) == 0)
    def _():
        me = me_ref[0]
        total = jnp.zeros((8, D), f32)
        up_bias = jnp.zeros((8, D), f32)
        for (core, y, x), piece in zip(PIECES, pieces):
            for z in range(piece.shape[0]):
                group = (16 * y + 8 * core + 2 * z + x) ^ me
                for part in range(4):
                    scr[part, group] = piece[z, part * ROWS : (part + 1) * ROWS, :]
                total = total + piece[z, 4 * ROWS : 4 * ROWS + 8, :].astype(f32)
                up_bias = up_bias + piece[z, 4 * ROWS + 8 : 4 * ROWS + 16, :].astype(f32)
        vec_ref[...] = total
        upb_ref[...] = up_bias
        for part in range(3):
            w_ref[part] = scr[part].reshape(D, D)
        out_ref[...] = dot_tn(order_ref[...], scr[3].reshape(D, D)).astype(bf16)

    own, other = x_ref[...], xp_ref[...]
    q_ref[...] = (dot_nn(own, w_ref[0]) + vec_ref[0:1, :]).astype(bf16)
    k_ref[:, :HALF] = dot_nn(other, w_ref[1, :, :HALF]).astype(bf16)
    k_ref[:, HALF:] = dot_nn(own, w_ref[1, :, HALF:]).astype(bf16)
    v_ref[:, :HALF] = (dot_nn(other, w_ref[2, :, :HALF]) + vec_ref[1:2, :HALF]).astype(bf16)
    v_ref[:, HALF:] = (dot_nn(own, w_ref[2, :, HALF:]) + vec_ref[1:2, HALF:]).astype(bf16)


def project(me, x, xp, pieces, order):
    rows = x.shape[0]
    step = BLOCK
    row_spec = pl.BlockSpec((step, D), lambda i, *_: (i, 0))
    return call(
        project_body,
        (rows // step,),
        [row_spec, row_spec] + [whole(pieces[0].shape)] * len(PIECES) + [whole((D, D))],
        [row_spec] * 3 + [whole((3, D, D)), whole((D, D)), whole((8, D)), whole((8, D))],
        [sds((rows, D), bf16)] * 3 + [sds((3, D, D), bf16), sds((D, D), bf16), sds((8, D), f32), sds((8, D), f32)],
        scratch=[pltpu.VMEM((4, GROUPS_W, ROWS, D), bf16)],
        prefetch=1,
        flops=6 * rows * D * D,
        moved=10 * rows * D + 12 * D * D,
        name="project",
    )(me, x, xp, *pieces, order)


def attend_body(valid_ref, q_ref, k_ref, v_ref, ctx_ref, p_ref):
    seq, pair = pl.program_id(0), pl.program_id(1)
    valid = valid_ref[seq, pair // 3]
    queries, keys, values = q_ref[...], k_ref[...], v_ref[...]
    lane = lax.broadcasted_iota(jnp.int32, (BLOCK, PAIR), 1)
    key_row = lax.broadcasted_iota(jnp.int32, (BLOCK, 1), 0)
    fill = jnp.where(key_row < valid, 0.0, masked_fill * LOG2E)
    parts = []
    for head in range(2):
        mine = (lane < HD) if head == 0 else (lane >= HD)
        masked = jnp.where(mine, queries, jnp.zeros_like(queries))
        scores = dot_nt(keys, masked) * (LOG2E * HD ** (-0.5)) + fill
        top = jnp.max(scores, axis=0, keepdims=True)
        weights = jnp.exp2(scores - top)
        total = jnp.sum(weights, axis=0, keepdims=True)
        probs = (weights * (1.0 / total)).astype(bf16)
        p_ref[0, head] = probs
        parts.append(dot_tn(probs, values))
    ctx_ref[...] = jnp.where(lane < HD, parts[0], parts[1]).astype(bf16)


def attend(valid, q, k, v):
    rows = q.shape[0]
    seqs = rows // BLOCK
    spec = pl.BlockSpec((BLOCK, PAIR), lambda s, j, *_: (s, j))
    return call(
        attend_body,
        (seqs, H // 2),
        [spec] * 3,
        [spec, pl.BlockSpec((1, 2, BLOCK, BLOCK), lambda s, j, *_: (s, j, 0, 0))],
        [sds((rows, D), bf16), sds((seqs, H, BLOCK, BLOCK), bf16)],
        prefetch=1,
        flops=16 * rows * BLOCK * D,
        moved=8 * rows * D + 2 * rows * H * BLOCK,
        name="attend",
    )(valid, q, k, v)


def attend_back_body(q_ref, k_ref, v_ref, p_ref, gctx_ref, out_ref, give_ref):
    pair = pl.program_id(1)
    queries, keys, values, grad_ctx = q_ref[...], k_ref[...], v_ref[...], gctx_ref[...]
    lane = lax.broadcasted_iota(jnp.int32, (BLOCK, PAIR), 1)
    scale = HD ** (-0.5)
    gq, gk, gv = [], [], []
    for head in range(2):
        mine = (lane < HD) if head == 0 else (lane >= HD)
        probs = p_ref[0, head]
        grad_probs = dot_nt(jnp.where(mine, values, jnp.zeros_like(values)), grad_ctx)
        delta = jnp.sum(probs.astype(f32) * grad_probs, axis=0, keepdims=True)
        grad_scores = (probs.astype(f32) * (grad_probs - delta)).astype(bf16)
        gv.append(dot_nn(probs, grad_ctx))
        gk.append(dot_nn(grad_scores, queries))
        gq.append(dot_tn(grad_scores, keys))
    first = lane < HD
    out_ref[0] = (jnp.where(first, gq[0], gq[1]) * scale).astype(bf16)
    grad_keys = (jnp.where(first, gk[0], gk[1]) * scale).astype(bf16)
    grad_values = jnp.where(first, gv[0], gv[1]).astype(bf16)
    out_ref[1] = grad_keys
    out_ref[2] = grad_values

    @pl.when(pair < H // 4)
    def _():
        give_ref[0] = grad_keys
        give_ref[1] = grad_values


def attend_back(q, k, v, probs, grad_ctx):
    rows = q.shape[0]
    seqs = rows // BLOCK
    spec = pl.BlockSpec((BLOCK, PAIR), lambda s, j: (s, j))
    return call(
        attend_back_body,
        (seqs, H // 2),
        [spec] * 3
        + [
            pl.BlockSpec((1, 2, BLOCK, BLOCK), lambda s, j: (s, j, 0, 0)),
            spec,
        ],
        [
            pl.BlockSpec((3, BLOCK, PAIR), lambda s, j: (0, s, j)),
            pl.BlockSpec((2, BLOCK, PAIR), lambda s, j: (0, s, jnp.minimum(j, H // 4 - 1))),
        ],
        [sds((3, rows, D), bf16), sds((2, rows, HALF), bf16)],
        flops=32 * rows * BLOCK * D,
        moved=14 * rows * D + 2 * rows * H * BLOCK,
        name="attend_back",
    )(q, k, v, probs, grad_ctx)


def mean_last(value):
    return jnp.sum(value, axis=-1, keepdims=True) * (1.0 / D)


def first_norm_body(ctx_ref, x_ref, wop_ref, vec_ref, hat_ref, inv_ref, low_ref):
    branch = dot_nn(ctx_ref[...], wop_ref[...]) + vec_ref[2:3, :]
    residual = x_ref[...].astype(f32) + branch
    centred = residual - mean_last(residual)
    inv = lax.rsqrt(mean_last(centred * centred) + norm_eps)
    hat = centred * inv
    hat_ref[...] = hat
    inv_ref[...] = jnp.broadcast_to(inv, inv_ref.shape)
    low_ref[...] = (hat * vec_ref[3:4, :] + vec_ref[4:5, :]).astype(bf16)


def first_norm(ctx, x, wop, vecs):
    rows = x.shape[0]
    step = BLOCK
    row_spec = pl.BlockSpec((step, D), lambda i: (i, 0))
    return call(
        first_norm_body,
        (rows // step,),
        [row_spec, row_spec, whole((D, D)), whole((8, D))],
        [row_spec, pl.BlockSpec((step, LANES), lambda i: (i, 0)), row_spec],
        [sds((rows, D), f32), sds((rows, LANES), f32), sds((rows, D), bf16)],
        flops=2 * rows * D * D,
        moved=12 * rows * D,
        name="first_norm",
    )(ctx, x, wop, vecs)


def gelu_and_slope(value):
    size = jnp.abs(value)
    gauss = jnp.exp2(value * value * (-0.5 * LOG2E))
    knot = 1.0 / (1.0 + size * (0.3275911 * SQRT_HALF))
    poly = knot * (
        0.254829592 + knot * (-0.284496736 + knot * (1.421413741 + knot * (-1.453152027 + knot * 1.061405429)))
    )
    tail = 0.5 * poly * gauss
    normal_cdf = jnp.where(value >= 0.0, 1.0 - tail, tail)
    return value * normal_cdf, normal_cdf + value * gauss * INV_SQRT_2PI


def ffn_forward_body(
    low_ref, hat_ref, cot_ref, up_ref, down_ref, bias_ref, vec_ref,
    act_ref, slope_ref, out_ref, gtwo_ref, gsec_ref, sums_ref, acc,
):
    chunk, last = pl.program_id(1), pl.num_programs(1) - 1
    first = (pl.program_id(0) == 0) & (chunk == 0)
    rows = low_ref.shape[0]
    step = 256
    w_up = square(up_ref)
    w_down = square(down_ref)

    @pl.when(first)
    def _():
        sums_ref[...] = jnp.zeros_like(sums_ref)

    @pl.when(chunk == 0)
    def _():
        acc[...] = jnp.zeros_like(acc)

    for start in range(0, rows, step):
        part = pl.ds(start, step)
        hidden = dot_nn(low_ref[part, :], w_up) + bias_ref[pl.ds(chunk, 1), :]
        activated, slope = gelu_and_slope(hidden)
        activated = activated.astype(bf16)
        act_ref[part, :] = activated
        slope_ref[part, :] = slope.astype(bf16)
        down = dot_nn(activated, w_down)

        acc[part, :] += down

    @pl.when(chunk == last)
    def _():
        gain, bias = vec_ref[6:7, :], vec_ref[7:8, :]

        def rows_of(index, sums):
            part = pl.ds(pl.multiple_of(index * step, step), step)
            residual = hat_ref[part, :] * vec_ref[3:4, :] + vec_ref[4:5, :] + (acc[part, :] + vec_ref[5:6, :])
            centred = residual - mean_last(residual)
            inv = lax.rsqrt(mean_last(centred * centred) + norm_eps)
            hat = centred * inv
            out_ref[part, :] = (hat * gain + bias).astype(bf16)
            cot = cot_ref[part, :].astype(f32)
            scaled = cot * gain
            grad = inv * (scaled - mean_last(scaled) - hat * mean_last(scaled * hat))
            gtwo_ref[part, :] = grad
            low = grad.astype(bf16)
            gsec_ref[part, :] = low
            return (
                sums[0] + jnp.sum(cot * hat, axis=0, keepdims=True),
                sums[1] + jnp.sum(cot, axis=0, keepdims=True),
                sums[2] + jnp.sum(low.astype(f32), axis=0, keepdims=True),
            )

        zero = jnp.zeros((1, D), f32)
        sums = lax.fori_loop(0, rows // step, rows_of, (zero, zero, zero))
        for index, value in enumerate(sums):
            sums_ref[index : index + 1, :] += value


def ffn_forward(low, hat, cot, pack, up_bias, vecs):
    rows = low.shape[0]
    span = 1024
    chunks = FF // D
    row_spec = pl.BlockSpec((span, D), lambda r, c: (r, 0))
    wide = pl.BlockSpec((span, D), lambda r, c: (r, c))
    return call(
        ffn_forward_body,
        (rows // span, chunks),
        [
            row_spec,
            row_spec,
            row_spec,
            pl.BlockSpec((GROUPS_W, ROWS, D), lambda r, c: (0, 4 + c, 0)),
            pl.BlockSpec((GROUPS_W // 4, 4 * ROWS, D), lambda r, c: (c, 0, 0)),
            whole((8, D)),
            whole((8, D)),
        ],
        [wide, wide, row_spec, row_spec, row_spec, whole((8, D))],
        [
            sds((rows, FF), bf16),
            sds((rows, FF), bf16),
            sds((rows, D), bf16),
            sds((rows, D), f32),
            sds((rows, D), bf16),
            sds((8, D), f32),
        ],
        scratch=[pltpu.VMEM((span, D), f32)],
        flops=4 * rows * D * FF,
        moved=26 * rows * D + 4 * D * FF,
        name="ffn_forward",
    )(low, hat, cot, pack, pack, up_bias, vecs)


def grad_down_body(me_ref, act_ref, gsec_ref, keep_ref, send_ref, scr):
    step = pl.program_id(0)
    scr[...] = dot_tn(act_ref[...], gsec_ref[...]).astype(bf16).reshape(scr.shape)
    place = jnp.bitwise_and(me_ref[0], 7)

    @pl.when(step < 2)
    def _():
        for index in range(8):
            keep_ref[0, index] = scr[place ^ index]

    @pl.when(step >= 2)
    def _():
        for index in range(8):
            send_ref[0, index] = scr[place ^ index]


def grad_down_of(me, act, gsec):
    rows = act.shape[0]
    block = (1, GROUPS_W // 4, 4 * ROWS, D)
    return call(
        grad_down_body,
        (FF // D,),
        [
            pl.BlockSpec((rows, D), lambda s, me_ref: (0, ((s % 2) * 2 + s // 2) ^ (me_ref[0] // 8))),
            whole((rows, D)),
        ],
        [
            pl.BlockSpec(block, lambda s, me_ref: (jnp.minimum(s, 1), 0, 0, 0)),
            pl.BlockSpec(block, lambda s, me_ref: (jnp.maximum(s - 2, 0), 0, 0, 0)),
        ],
        [sds((2, *block[1:]), bf16)] * 2,
        scratch=[pltpu.VMEM(block[1:], bf16)],
        prefetch=1,
        flops=2 * rows * D * FF,
        moved=10 * rows * D + 2 * D * FF,
        name="grad_down",
    )(me, act, gsec)


def apart(scr, me, keep, send):
    for index in range(GROUPS_W // 2):
        group = me ^ (2 * index - index % 8)
        keep(index, scr[group])
        send(index, scr[group ^ 8])


def ffn_backward_body(
    me_ref, gsec_ref, slope_ref, low_ref, up_ref, down_ref, keep_ref, send_ref, gbias_ref, acc_ref, scr
):
    chunk = pl.program_id(0)
    grad_act = dot_nt(gsec_ref[...], square(down_ref))
    grad_hidden = (grad_act * slope_ref[...].astype(f32)).astype(bf16)
    gbias_ref[0] = jnp.sum(grad_hidden.astype(f32), axis=0, keepdims=True)
    scr[...] = dot_tn(low_ref[...], grad_hidden).astype(bf16).reshape(scr.shape)

    def keep(index, value):
        keep_ref[index] = value

    def send(index, value):
        send_ref[index] = value

    apart(scr, me_ref[0], keep, send)
    back = dot_nt(grad_hidden, square(up_ref))

    @pl.when(chunk == 0)
    def _():
        acc_ref[...] = back

    @pl.when(chunk > 0)
    def _():
        acc_ref[...] += back


def ffn_backward(me, gsec, slope, low, pack):
    rows = gsec.shape[0]
    half = pl.BlockSpec((GROUPS_W // 2, ROWS, D), lambda c, *_: (0, c, 0))
    return call(
        ffn_backward_body,
        (FF // D,),
        [
            whole((rows, D)),
            pl.BlockSpec((rows, D), lambda c, *_: (0, c)),
            whole((rows, D)),
            pl.BlockSpec((GROUPS_W, ROWS, D), lambda c, *_: (0, 4 + c, 0)),
            pl.BlockSpec((GROUPS_W // 4, 4 * ROWS, D), lambda c, *_: (c, 0, 0)),
        ],
        [half, half, pl.BlockSpec((1, 1, D), lambda c, *_: (c, 0, 0)), whole((rows, D))],
        [sds((GROUPS_W // 2, 4 * ROWS, D), bf16)] * 2 + [sds((FF // D, 1, D), f32), sds((rows, D), f32)],
        scratch=[pltpu.VMEM((GROUPS_W, ROWS, D), bf16)],
        prefetch=1,
        flops=6 * rows * D * FF,
        moved=16 * rows * D + 6 * D * FF,
        name="ffn_backward",
    )(me, gsec, slope, low, pack, pack)


def first_back_body(
    acc_ref, gtwo_ref, hat_ref, inv_ref, ctx_ref, wop_ref, order_ref, vec_ref,
    gres_ref, gctx_ref, gout_ref, sums_ref, gout_scr,
):
    index, last = pl.program_id(0), pl.num_programs(0) - 1
    hat = hat_ref[...]
    inv = inv_ref[:, 0:1]
    grad_first = gtwo_ref[...] + acc_ref[...]
    scaled = grad_first * vec_ref[3:4, :]
    grad = inv * (scaled - mean_last(scaled) - hat * mean_last(scaled * hat))
    gres_ref[...] = grad
    low = grad.astype(bf16)
    ctx = ctx_ref[...]
    gctx_ref[...] = dot_nt(low, wop_ref[...]).astype(bf16)
    grad_out = dot_tn(ctx, low)

    @pl.when(index == 0)
    def _():
        gout_scr[...] = grad_out
        sums_ref[...] = jnp.zeros_like(sums_ref)

    @pl.when(index > 0)
    def _():
        gout_scr[...] += grad_out

    sums_ref[0:1, :] += jnp.sum(grad_first * hat, axis=0, keepdims=True)
    sums_ref[1:2, :] += jnp.sum(grad_first, axis=0, keepdims=True)
    sums_ref[2:3, :] += jnp.sum(low.astype(f32), axis=0, keepdims=True)

    @pl.when(index == last)
    def _():
        ordered = dot_nn(order_ref[...], gout_scr[...].astype(bf16))
        gout_ref[...] = ordered.astype(bf16).reshape(gout_ref.shape)


def first_back(acc, gtwo, hat, inv, ctx, wop, order, vecs):
    rows = acc.shape[0]
    step = 2 * BLOCK
    row_spec = pl.BlockSpec((step, D), lambda i: (i, 0))
    return call(
        first_back_body,
        (rows // step,),
        [
            row_spec,
            row_spec,
            row_spec,
            pl.BlockSpec((step, LANES), lambda i: (i, 0)),
            row_spec,
            whole((D, D)),
            whole((D, D)),
            whole((8, D)),
        ],
        [
            row_spec,
            row_spec,
            whole((GROUPS_W, ROWS, D)),
            whole((8, D)),
        ],
        [
            sds((rows, D), f32),
            sds((rows, D), bf16),
            sds((GROUPS_W, ROWS, D), bf16),
            sds((8, D), f32),
        ],
        scratch=[pltpu.VMEM((D, D), f32)],
        flops=4 * rows * D * D,
        moved=20 * rows * D + 6 * D * D,
        name="first_back",
    )(acc, gtwo, hat, inv, ctx, wop, order, vecs)


def in_order(rows, order):
    high = rows.astype(bf16)
    rest = rows - high.astype(f32)
    middle = rest.astype(bf16)
    low = (rest - middle.astype(f32)).astype(bf16)
    return dot_nt(high, order) + (dot_nt(middle, order) + dot_nt(low, order))


LAST_ROWS = 4 * ROWS + 8
N_VEC = 8 * D // GROUPS_W
N_BIAS = FF // GROUPS_W


def grad_project_body(
    me_ref, x_ref, xp_ref, grad_ref, gout_ref, one_ref, two_ref, upb_ref, order_ref, keep_ref, send_ref, scr, sums, small
):
    part = pl.program_id(0)
    me = me_ref[0]
    own = x_ref[...]
    other = jnp.where(part == 0, own, xp_ref[...])
    grad = grad_ref[0]
    left = dot_tn(other, grad[:, :HALF]).astype(bf16)
    right = dot_tn(own, grad[:, HALF:]).astype(bf16)
    scr[:, :, :HALF] = left.reshape(GROUPS_W, ROWS, HALF)
    scr[:, :, HALF:] = right.reshape(GROUPS_W, ROWS, HALF)
    sums[pl.ds(part, 1), :] = jnp.sum(grad.astype(f32), axis=0, keepdims=True)

    def place(source, start, size):
        def keep(index, value):
            keep_ref[index, start : start + size, :] = value.astype(bf16)

        def send(index, value):
            send_ref[index, start : start + size, :] = value.astype(bf16)

        apart(source, me, keep, send)

    for index in range(3):

        @pl.when(part == index)
        def _():
            place(scr, (index + 1) * ROWS, ROWS)

    @pl.when(part == 0)
    def _():
        place(gout_ref, 0, ROWS)

    @pl.when(part == 2)
    def _():
        bias = in_order(sums[...], order_ref[...])
        rows = (
            bias[0:1], bias[2:3], one_ref[2:3, :], one_ref[0:1, :],
            one_ref[1:2, :], two_ref[2:3, :], two_ref[0:1, :], two_ref[1:2, :],
        )
        small[...] = jnp.zeros_like(small)
        for group in range(GROUPS_W):
            row, column = divmod(group, GROUPS_W // 8)
            small[group, 0:1, :N_VEC] = rows[row][:, column * N_VEC : (column + 1) * N_VEC]
            row, column = divmod(group, GROUPS_W // 4)
            small[group, 0:1, N_VEC : N_VEC + N_BIAS] = upb_ref[row, :, column * N_BIAS : (column + 1) * N_BIAS]
        place(small, 4 * ROWS, 8)


def grad_project(me, x, xp, grads, grad_out, sums_one, sums_two, up_bias, order):
    rows = x.shape[0]
    half = (GROUPS_W // 2, LAST_ROWS, D)
    return call(
        grad_project_body,
        (3,),
        [
            whole((rows, D)),
            whole((rows, D)),
            pl.BlockSpec((1, rows, D), lambda s, *_: (s, 0, 0)),
            whole((GROUPS_W, ROWS, D)),
            whole((8, D)),
            whole((8, D)),
            whole((FF // D, 1, D)),
            whole((D, D)),
        ],
        [whole(half)] * 2,
        [sds(half, bf16)] * 2,
        scratch=[
            pltpu.VMEM((GROUPS_W, ROWS, D), bf16),
            pltpu.VMEM((8, D), f32),
            pltpu.VMEM((GROUPS_W, 8, D), f32),
        ],
        prefetch=1,
        flops=6 * rows * D * D,
        moved=10 * rows * D + 12 * D * D,
        name="grad_project",
    )(me, x, xp, grads, grad_out, sums_one, sums_two, up_bias, order)


def grad_input_body(gres_ref, grads_ref, back_ref, w_ref, out_ref):
    total = gres_ref[...] + dot_nt(grads_ref[0], w_ref[0])
    for part in (1, 2):
        total = total + dot_nt(back_ref[part - 1], w_ref[part, :, :HALF])
        total = total + dot_nt(grads_ref[part, :, HALF:], w_ref[part, :, HALF:])
    out_ref[...] = total


def grad_input_of(gres, grads, back, weights):
    rows = gres.shape[0]
    step = 256
    row_spec = pl.BlockSpec((step, D), lambda i: (i, 0))
    return call(
        grad_input_body,
        (rows // step,),
        [
            row_spec,
            pl.BlockSpec((3, step, D), lambda i: (0, i, 0)),
            pl.BlockSpec((2, step, HALF), lambda i: (0, i, 0)),
            whole((3, D, D)),
        ],
        row_spec,
        sds((rows, D), f32),
        flops=6 * rows * D * D,
        moved=16 * rows * D + 6 * D * D,
        name="grad_input",
    )(gres, grads, back, weights)


def summed(refs, start, stop):
    total = refs[0][start:stop, :].astype(f32)
    for ref in refs[1:]:
        total = total + ref[start:stop, :].astype(f32)
    return total


def spread(out_ref, total, first, stride):
    for column in range(D // LANES):
        out_ref[pl.ds(first + column, total.shape[0], stride=stride), :] = total[:, column * LANES : (column + 1) * LANES]


def finish_ffn_body(*refs):
    up_ref, down_ref = refs[6:]
    for chunk in range(4):
        spread(up_ref, summed(refs[:3], chunk * ROWS, (chunk + 1) * ROWS), chunk * (D // LANES), FF // LANES)
    spread(down_ref, summed(refs[3:6], 0, 4 * ROWS), 0, D // LANES)


def finish_last_body(*refs):
    order_ref, out_ref, q_ref, k_ref, v_ref, vec_ref, upb_ref = refs[6:]
    one, two = refs[:3], refs[3:6]
    half = one[0].shape[0]
    spread(out_ref, summed(one, 0, ROWS), 0, D // LANES)
    middle = jnp.concatenate((summed(one, ROWS, half), summed(two, 0, 4 * ROWS - half)), axis=0)
    ordered = in_order(middle, order_ref[...])
    for part, ref in enumerate((q_ref, k_ref, v_ref)):
        spread(ref, ordered[part * ROWS : (part + 1) * ROWS], 0, D // LANES)
    small = summed(two, 4 * ROWS - half, 4 * ROWS - half + 8)
    vec_ref[...] = small[0, :N_VEC]
    upb_ref[...] = small[0, N_VEC : N_VEC + N_BIAS]


def z_first(one, two):
    return swap(one[1:3], "dp", 2), swap(two[2:4], "dp", 6)


def z_second(one, two, got_one, got_two):
    return swap(one[3] + got_one[1], "dp", 6), swap(two[1] + got_two[0], "dp", 2)


def finish(body, one, two, got, last, extra, sizes, name):
    shapes = [(size * D // LANES, LANES) for size in sizes]
    if extra:
        shapes = shapes + [(N_VEC,), (N_BIAS,)]

    def piece(value, index):
        return pl.BlockSpec((None, *value.shape[1:]), lambda i: (index, 0, 0))

    return call(
        body,
        (1,),
        [piece(one, 0), piece(got[0], 0), whole(last[0].shape), piece(two, 0), piece(got[1], 1), whole(last[1].shape)]
        + [whole(value.shape) for value in extra],
        [whole(shape) for shape in shapes],
        [sds(shape, f32) for shape in shapes],
        moved=8 * (one.shape[1] + two.shape[1]) * D,
        name=name,
    )(one, got[0], last[0], two, got[1], last[1], *extra)


def gather(value):
    return lax.all_gather(value, BOTH, axis=0)


def scatter(value):
    return lax.psum_scatter(value, BOTH, scatter_dimension=0)


def joined(gathered, start, rows, columns=1):
    count = gathered.shape[0]
    part = gathered[:, start : start + columns * rows]
    if columns > 1:
        part = part.reshape(GROUPS_W, count // GROUPS_W, columns, rows, D).transpose(0, 2, 1, 3, 4)
    return part.reshape(GROUPS_W, -1, D)


def parted(grouped, count, rows, columns=1):
    if columns > 1:
        grouped = grouped.reshape(GROUPS_W, columns, count // GROUPS_W, rows, D).transpose(0, 2, 1, 3, 4)
    return grouped.reshape(count, columns * rows, D)


def gather_near(shard):
    rows = shard.shape[0]
    half = rows // 16 * 8
    one, three = swap(shard, "dp", 2), swap(shard, "dp", 6)
    two = jnp.concatenate((swap(three[:half], "dp", 2), swap(one[half:], "dp", 6)))
    column = jnp.stack((shard, one, two, three))
    over_x = swap(column, "dp", 1)
    over_y = swap(column, "blk", 2)
    over_both = jnp.concatenate((swap(over_y[:, :half], "dp", 1), swap(over_x[:, half:], "blk", 2)), axis=1)
    near = {(0, 0): column, (0, 1): over_x, (1, 0): over_y, (1, 1): over_both}
    pieces = {(0, y, x): value for (y, x), value in near.items()}
    pieces.update({(1, y, x): swap(value, "blk", 1) for (y, x), value in near.items()})
    return [pieces[key] for key in PIECES]


def over_cores(keep, received):
    return (keep + received).reshape(2, 4, 2, keep.shape[1], D)


def over_x(total):
    return total[:, :, 0] + swap(total[:, :, 1], "dp", 1)


def over_y(total):
    return total[0] + swap(total[1], "blk", 2)


def over_first(total):
    rows = total.shape[3]
    half = (rows + 8) // 16 * 8
    one, two = total[:, :, :, :half], total[:, :, :, half:]
    return one[:, :, 0] + swap(one[:, :, 1], "dp", 1), two[0] + swap(two[1], "blk", 2)


def over_second(pair):
    one, two = pair
    one = one[0] + swap(one[1], "blk", 2)
    two = two[:, 0] + swap(two[:, 1], "dp", 1)
    return one, two


def together(*values):
    return lax.optimization_barrier(values)


def every_group(keep, send):
    rows = keep.shape[1]
    return jnp.stack((keep.reshape(2, 8, rows, D), send.reshape(2, 8, rows, D)), axis=1).reshape(GROUPS_W, rows, D)


def body(tokens, cotangent, lengths, head_mode, w_query, w_key, w_value, w_out, w_up, w_down, b_up, vectors):
    seq_count = tokens.shape[0]
    row_count = seq_count * BLOCK
    devices = lax.axis_size("blk") * lax.axis_size("dp")
    near = devices == GROUPS_W
    own_rows = D // devices
    n_vec, n_bias = vectors.shape[0], b_up.shape[0]
    blk_index = lax.axis_index("blk")
    device = blk_index * lax.axis_size("dp") + lax.axis_index("dp")
    me = (device if near else device * 0).reshape(1).astype(jnp.int32)
    block_side = blk_index % 2
    member = blk_index // 2
    seq_lengths = jnp.where(member == 0, lengths[:, 0], lengths[:, 1])
    valid = jnp.stack(
        (
            jnp.clip(seq_lengths - (1 - block_side) * BLOCK, 0, BLOCK),
            jnp.clip(seq_lengths - block_side * BLOCK, 0, BLOCK),
        ),
        axis=1,
    ).astype(jnp.int32)
    swapped = head_mode == 1
    place = jnp.where(swapped, jnp.cumsum(swapped) - 1, H // 2 + jnp.cumsum(~swapped) - 1)
    target = jnp.repeat(place * HD, HD) + jnp.tile(jnp.arange(HD), H)
    order = (target[:, None] == jnp.arange(D)[None, :]).astype(bf16)

    inputs = tokens.reshape(row_count, D)
    other_inputs = swap(inputs, "blk", 1)

    ffn_shard = jnp.concatenate(
        (
            w_down.reshape(4 * own_rows, D),
            w_up.reshape(own_rows, 4, D).transpose(1, 0, 2).reshape(4 * own_rows, D),
        )
    )
    ffn_pack = gather(ffn_shard)
    up_bias = lax.dynamic_update_slice(jnp.zeros((8 * D,), bf16), b_up, (device * n_bias,)).reshape(8, D)
    small = lax.dynamic_update_slice(jnp.zeros((8 * D,), bf16), vectors, (device * n_vec,)).reshape(8, D)
    stacked = jnp.concatenate([w.reshape(own_rows, D) for w in (w_query, w_key, w_value)] + [small[0:2]])
    stacked = dot_nn(stacked, order).astype(bf16)
    attn_shard = jnp.concatenate(
        (stacked[: 3 * own_rows], w_out.reshape(own_rows, D), stacked[3 * own_rows :], small[2:], up_bias)
    )
    if near:
        pieces = gather_near(attn_shard)
    else:
        attn_all = gather(attn_shard)
        attn_pack = jnp.concatenate(
            [joined(attn_all, s * own_rows, own_rows) for s in range(4)]
            + [jnp.sum(attn_all[:, 4 * own_rows :].reshape(GROUPS_W, -1, 16, D), axis=1)],
            axis=1,
        ).reshape(2, 2, 4, 2, 4 * ROWS + 16, D)
        pieces = [attn_pack[y, core, :, x] for core, y, x in PIECES]
        ffn_pack = jnp.concatenate(
            (joined(ffn_pack, 0, 4 * own_rows), joined(ffn_pack, 4 * own_rows, own_rows, 4)), axis=1
        )

    q, k, v, attn_weights, out_weight, vecs, up_biases = project(me, inputs, other_inputs, pieces, order)
    ctx, probs = attend(valid, q, k, v)
    hat, inv, low = first_norm(ctx, inputs, out_weight, vecs)
    act, slope, output, gtwo, gsec, sums_two = ffn_forward(
        low, hat, cotangent.reshape(row_count, D), ffn_pack, up_biases, vecs
    )
    down_keep, down_send = grad_down_of(me, act, gsec)
    down_keep, down_send = (value.reshape(GROUPS_W // 2, 4 * ROWS, D) for value in (down_keep, down_send))
    down_keep, down_send, gsec = together(down_keep, down_send, gsec)
    up_keep, up_send, grad_up_bias, acc = ffn_backward(me, gsec, slope, low, ffn_pack)
    if near:
        received, acc = together(swap(down_send, "blk", 1), acc)
        down = over_cores(down_keep, received)
    gres, grad_ctx, grad_out, sums_one = first_back(acc, gtwo, hat, inv, ctx, out_weight, order, vecs)
    if near:
        received, grad_ctx = together(swap(up_send, "blk", 1), grad_ctx)
        up = over_cores(up_keep, received)
    grads, give = attend_back(q, k, v, probs, grad_ctx)
    if near:
        up, down, grads, give = together(over_x(up), over_y(down), grads, give)
    back = swap(give, "blk", 1)
    last_keep, last_send = grad_project(
        me, inputs, other_inputs, grads, grad_out, sums_one, sums_two, grad_up_bias, order
    )
    if near:
        up, down, last_keep, last_send = together(
            over_y(up), down[:, 0] + swap(down[:, 1], "dp", 1), last_keep, last_send
        )
        received, gres = together(swap(last_send, "blk", 1), gres)
        last = over_cores(last_keep, received)
    grad_inputs = grad_input_of(gres, grads, back, attn_weights)
    outputs = (output.reshape(tokens.shape), grad_inputs.reshape(tokens.shape))

    if near:
        *got, grad_inputs = together(*z_first(up, down), grad_inputs)
        outputs = (output.reshape(tokens.shape), grad_inputs.reshape(tokens.shape))
        *pair, got_up, got_down = together(*over_first(last), *got)
        one, two, *ends = together(*over_second(pair), *z_second(up, down, got_up, got_down))
        up_sum, down_sum = finish(
            finish_ffn_body, up, down, (got_up, got_down), ends, (), (4 * ROWS, 4 * ROWS), "finish_ffn"
        )
        *got, up_sum = together(*z_first(one, two), up_sum)
        out_sum, query_sum, key_sum, value_sum, vec_sum, bias_sum = finish(
            finish_last_body, one, two, got, z_second(one, two, *got), (order,), (ROWS,) * 4, "finish_last"
        )
        return (
            *outputs,
            query_sum.reshape(-1),
            key_sum.reshape(-1),
            value_sum.reshape(-1),
            out_sum.reshape(-1),
            up_sum.reshape(-1),
            down_sum.reshape(-1),
            bias_sum,
            vec_sum,
        )
    down_sum = scatter(parted(every_group(down_keep, down_send), devices, 4 * own_rows)).astype(f32)
    up_sum = scatter(parted(every_group(up_keep, up_send), devices, own_rows, 4)).astype(f32)
    last = every_group(last_keep, last_send)
    tail = jnp.concatenate(
        (
            last[:, 4 * ROWS, :N_VEC].reshape(devices, n_vec),
            last[:, 4 * ROWS, N_VEC : N_VEC + N_BIAS].reshape(devices, n_bias),
        ),
        axis=1,
    )
    tail = jnp.pad(tail, ((0, 0), (0, D - n_vec - n_bias)))[:, None, :]
    last_sum = scatter(
        jnp.concatenate([parted(last[:, s * ROWS : (s + 1) * ROWS], devices, own_rows) for s in range(4)] + [tail], axis=1)
    ).astype(f32)
    qkv_sum = lax.dot_general(
        last_sum[own_rows : 4 * own_rows],
        order.astype(f32),
        (((1,), (1,)), ((), ())),
        precision=lax.Precision.HIGHEST,
    ).reshape(3, own_rows * D)
    small_sum = last_sum[4 * own_rows]
    return (
        *outputs,
        qkv_sum[0],
        qkv_sum[1],
        qkv_sum[2],
        last_sum[:own_rows].reshape(-1),
        up_sum.reshape(4, own_rows, D).transpose(1, 0, 2).reshape(-1),
        down_sum.reshape(-1),
        small_sum[n_vec : n_vec + n_bias],
        small_sum[:n_vec],
    )


def solution(mesh):
    flat = P(BOTH)
    block = P("dp", "blk", None, None)
    return jax.shard_map(
        body,
        mesh=mesh,
        in_specs=(block, block, P("dp", None), P(), *([flat] * 8)),
        out_specs=(block, block, *([flat] * 8)),
        check_vma=False,
    )
```
